32 devices in a mesh: subset: 4 (over x, core), slab: 8 (over z, y).
Axes of the slice: x: 2, y: 2, z: 4, core: 2. Of those that a mesh axis runs over, the one named last changes fastest.
Arguments:
- sinogram: bfloat16 [64, 64, 2048], P(('subset', 'slab')), may hold values from -12 to 12
- angles: float32 [64], P(('subset', 'slab')), may hold values from -3.140625 to 3.140625
- w_first: float32 [32, 27], replicated, may hold values from -1.25 to 1.25
- b_first: float32 [32], replicated, may hold values from -3 to 3
- w_second: float32 [32, 27], replicated, may hold values from -0.21875 to 0.21875
- b_second: float32 [1], replicated, may hold values from -3 to 3
Outputs:
- prediction: float32 [4, 32, 8, 1024], P('subset', 'slab')
- target_slab: float32 [4, 32, 8, 1024], P('subset', 'slab')
- loss: float32 [], replicated
- grad_w_first: float32 [32, 27], replicated
- grad_b_first: float32 [32], replicated
- grad_w_second: float32 [32, 27], replicated
- grad_b_second: float32 [1], replicated
The draws below stay inside these ranges and needn't reach their ends.
All inputs are finite; a program needn't handle non-finite values.
Results may differ from the reference program's by a relative error of at most 0.00065.
The reference program's roundings to bfloat16 on the way (of `weights`) count: a program that leaves them out, or rounds other values in their place, can miss the bound.
Values may be sent and summed in bfloat16 or wider, within the bound.
No kernel may reach another device: no remote copies, remote signals or barrier semaphores. Data moves between devices by JAX's collectives and lax.ppermute only.
A program may use at most 128 MiB of HBM per device.

```python
import math
import jax
import jax.numpy as jnp
from jax import lax

DET = 2048
CH = 32
X = 1024
Y = 8
Z = 64
SUBSETS = 2
VPS = 32
VIEWS = 64


def draw_sinogram(key, part):
    key_base = jax.random.fold_in(key, 11)
    view_scale = jnp.exp(jnp.log(3.0) * (jnp.arange(VIEWS, dtype=jnp.float32) / max(VIEWS - 1, 1) - 0.5))
    slice_scale = jnp.exp(jnp.log(3.0) * (jnp.arange(Z, dtype=jnp.float32) / max(Z - 1, 1) - 0.5))
    scales = view_scale[:, None, None] * slice_scale[None, :, None]
    base = jax.random.normal(key_base, (VIEWS, Z, DET), jnp.float32)
    values = base * scales
    return jnp.clip(values, -12.0, 12.0).astype(jnp.bfloat16)


def normal_values(stream_key, extent, spread, bound, held_as=jnp.bfloat16):
    values = jax.random.normal(stream_key, extent, jnp.float32) * spread
    return jnp.minimum(jnp.maximum(values, -bound), bound).astype(held_as)


def setup_inputs(seed: int = 0) -> dict:
    seeds = jax.random.split(jax.random.key(seed), 7)
    sinogram = draw_sinogram(jax.random.fold_in(seeds[6], 71), 0)
    angles = jnp.clip(jax.random.uniform(seeds[1], (VIEWS,), jnp.float32, -3.140625, 3.140625), -3.140625, 3.140625)
    w_first = normal_values(seeds[2], (CH, 27), 27 ** -0.5, 1.25, jnp.float32)
    b_first = normal_values(seeds[3], (CH,), 0.5, 3.0, jnp.float32)
    w_second = normal_values(seeds[4], (CH, 27), (27 * CH) ** -0.5, 0.21875, jnp.float32)
    b_second = normal_values(seeds[5], (1,), 0.5, 3.0, jnp.float32)
    return dict(sinogram=sinogram, angles=angles, w_first=w_first, b_first=b_first, w_second=w_second, b_second=b_second)


def make_patches(field_pad, depth):
    rows = field_pad.shape[1]
    cols = field_pad.shape[2]
    padded = jnp.pad(field_pad, ((0, 0), (1, 1), (1, 1)))
    pieces = []
    for shift_z in range(3):
        for shift_y in range(3):
            for shift_x in range(3):
                pieces.append(padded[shift_z:shift_z + depth, shift_y:shift_y + rows, shift_x:shift_x + cols].reshape(-1))
    return jnp.stack(pieces)

def conv_second(hidden_pad, w_second, depth, rows, cols):
    channels = hidden_pad.shape[0]
    taps = jnp.dot(w_second.T, hidden_pad.reshape(channels, -1), precision=lax.Precision.HIGHEST)
    taps = taps.reshape(27, depth + 2, rows + 2, cols + 2)
    added = jnp.zeros((depth, rows, cols), jnp.float32)
    for shift_z in range(3):
        for shift_y in range(3):
            for shift_x in range(3):
                added = added + taps[9 * shift_z + 3 * shift_y + shift_x, shift_z:shift_z + depth, shift_y:shift_y + rows, shift_x:shift_x + cols]
    return added

def network(params, inp):
    w_first, b_first, w_second, b_second = params
    channels = w_first.shape[0]
    inp_pad = jnp.pad(inp, ((1, 1), (0, 0), (0, 0)))
    patches = make_patches(inp_pad, Z)
    pre_act = jnp.dot(w_first, patches, precision=lax.Precision.HIGHEST) + b_first[:, None]
    hidden = jax.nn.relu(pre_act).reshape(channels, Z, Y, X)
    hidden_pad = jnp.pad(hidden, ((0, 0), (1, 1), (1, 1), (1, 1)))
    added = conv_second(hidden_pad, w_second, Z, Y, X)
    return inp + added + b_second[0]

def reference(sinogram, angles, w_first, b_first, w_second, b_second):
    subsets = SUBSETS
    group_views = VPS
    sino = sinogram.reshape(subsets, group_views, Z, DET)
    angle_rows = angles.reshape(subsets, group_views)
    columns = jnp.arange(X, dtype=jnp.float32) - (X - 1) / 2.0
    row_pos = jnp.arange(Y, dtype=jnp.float32) - (Y - 1) / 2.0

    def one_view(running, item):
        block_sino, block_angle = item
        positions = columns[None, None, :] * jnp.cos(block_angle)[:, None, None] + row_pos[None, :, None] * jnp.sin(block_angle)[:, None, None] + (DET - 1) / 2.0
        positions = positions.reshape(subsets, -1)
        lower = jnp.floor(positions)
        weight_low = jnp.maximum(0.0, 1.0 - jnp.abs(positions - lower)).astype(jnp.bfloat16)
        weight_high = jnp.maximum(0.0, 1.0 - jnp.abs(positions - (lower + 1.0))).astype(jnp.bfloat16)
        lower_index = jnp.clip(lower.astype(jnp.int32), 0, DET - 2)
        val_low = jnp.take_along_axis(block_sino, lower_index[:, None, :], axis=2)
        val_high = jnp.take_along_axis(block_sino, (lower_index + 1)[:, None, :], axis=2)
        contrib = weight_low[:, None, :].astype(jnp.float32) * val_low.astype(jnp.float32) + weight_high[:, None, :].astype(jnp.float32) * val_high.astype(jnp.float32)
        return (running + contrib, None)
    start = jnp.zeros((subsets, Z, Y * X), jnp.float32)
    summed, _ = lax.scan(one_view, start, (jnp.swapaxes(sino, 0, 1), angle_rows.T))
    recon = summed.reshape(subsets, Z, Y, X) * (math.pi / group_views)
    total = lax.optimization_barrier(jnp.sum(recon, axis=0))
    target = (total[None] - recon) / (subsets - 1)
    cells_all = float(subsets * Z * Y * X)
    params = (w_first, b_first, w_second, b_second)

    def per_subset(item):
        inp, tgt = item

        def loss_fn(weights):
            pred = network(weights, inp)
            return (jnp.sum((pred - tgt) ** 2) / cells_all, pred)
        value, grad_fn, pred = jax.vjp(loss_fn, params, has_aux=True)
        grads = grad_fn(jnp.float32(1.0))[0]
        return (pred, value, grads)
    preds, losses, grads = lax.map(per_subset, (recon, target))
    grads = jax.tree.map(lambda part: lax.optimization_barrier(jnp.sum(part, axis=0)), grads)
    preds_out = preds.reshape(subsets * 2, Z // 2, Y, X)
    target_out = target.reshape(subsets * 2, Z // 2, Y, X)
    return (preds_out, target_out, jnp.sum(losses), grads[0], grads[1], grads[2], grads[3])
```

```python
import functools
import math

import jax
import jax.numpy as jnp
from jax import lax
from jax.experimental import pallas as pl
from jax.experimental.pallas import tpu as pltpu
from jax.sharding import PartitionSpec as P

DET = 2048
X = 1024
Y = 8
LANES = 128
TAPS = 27
TILE = 256
BLOCK = 80
W_SECOND_AT = 32
B_SECOND_AT = 59
LOSS_AT = 64
GRAD_B_SECOND_AT = 65
HALO = 2
BOTH = ("subset", "slab")

RADIUS = math.hypot((X - 1) / 2.0, (Y - 1) / 2.0) + 0.25
FIRST_D = math.floor((DET - 1) / 2.0 - RADIUS)
LAST_D = math.floor((DET - 1) / 2.0 + RADIUS) + 1
D0 = FIRST_D // LANES * LANES
DW = -(-(LAST_D + 1 - D0) // LANES) * LANES
assert FIRST_D - D0 >= 6 and D0 + DW <= DET

F32 = jnp.float32
BF16 = jnp.bfloat16
VMEM = pl.BlockSpec(memory_space=pltpu.VMEM)
SMEM = pl.BlockSpec(memory_space=pltpu.SMEM)


def iota(shape, dim):
    return lax.broadcasted_iota(jnp.int32, shape, dim)


def split2(value):
    high = value.astype(BF16)
    return high, (value - high.astype(F32)).astype(BF16)


def dot(a, b):
    return jnp.dot(a, b, preferred_element_type=F32)


def dot_nt(a, b):
    return lax.dot_general(a, b, (((1,), (1,)), ((), ())), preferred_element_type=F32)


def pack_kernel(depth, trig_ref, sino_ref, out_ref, rows_ref):
    views, z_count = sino_ref.shape[0], sino_ref.shape[1]
    rows = depth + 2 * HALO
    lane = iota((rows, LANES), 1)
    zeros = jnp.zeros((8, DW), F32)
    for view in range(views):
        rows_ref[0:8, :] = zeros
        rows_ref[8 : 8 + z_count, :] = sino_ref[view, :, D0 : D0 + DW].astype(F32)
        rows_ref[8 + z_count : 16 + z_count, :] = zeros
        head = jnp.zeros((rows, LANES), F32)
        for which in range(2):
            left = jnp.full((rows, LANES), trig_ref[which, view], F32)
            for part in range(3):
                piece = left.astype(BF16).astype(F32)
                left = left - piece
                head = jnp.where(lane == 3 * which + part, piece, head)
        for to in range(out_ref.shape[0]):
            start = 8 + to * depth - HALO
            out_ref[to, view] = rows_ref[start : start + rows, :].astype(BF16)
            first = rows_ref[start : start + rows, 0:LANES]
            out_ref[to, view, :, 0:LANES] = jnp.where(lane < 6, head, first).astype(BF16)


def pack(trig, sino, group, depth):
    views, z_count = sino.shape[0], sino.shape[1]
    return pl.pallas_call(
        functools.partial(pack_kernel, depth),
        out_shape=jax.ShapeDtypeStruct((group, views, depth + 2 * HALO, DW), BF16),
        in_specs=[SMEM, VMEM],
        out_specs=VMEM,
        scratch_shapes=[pltpu.VMEM((z_count + 16, DW), F32)],
        name="pack",
    )(trig, sino)


def project_kernel(scale, data_ref, ext_ref, own_ref, low_ref, high_ref, tab_ref, scal_ref, sem):
    views, rows = data_ref.shape[0], data_ref.shape[1]
    centre = (DET - 1) / 2.0
    head = data_ref[:, 0, 0:LANES].astype(F32)
    cosine = jnp.broadcast_to(head[:, 0:1] + head[:, 1:2] + head[:, 2:3], (views, LANES))
    sine = jnp.broadcast_to(head[:, 3:4] + head[:, 4:5] + head[:, 5:6], (views, LANES))

    def at(col, row):
        return col * cosine + row * sine + centre

    start = (iota((views, LANES), 1) % (X // LANES)).astype(F32) * LANES - (X - 1) / 2.0
    stop = start + (LANES - 1.0)
    edge = (Y - 1) / 2.0
    least = jnp.minimum(
        jnp.minimum(at(start, -edge), at(stop, -edge)), jnp.minimum(at(start, edge), at(stop, edge))
    )
    tab_ref[0] = cosine
    tab_ref[1] = sine
    tab_ref[2] = ((jnp.floor(least).astype(jnp.int32) - D0) // LANES).astype(F32)
    copy = pltpu.make_async_copy(tab_ref, scal_ref, sem)
    copy.start()
    values = data_ref[...].astype(F32)
    low_ref[...] = values
    high_ref[...] = pltpu.roll(values.reshape(views * rows, DW), DW - 1, 1).reshape(values.shape)
    copy.wait()

    column = iota((Y, LANES), 1).astype(F32)
    row_pos = iota((Y, LANES), 0).astype(F32) - edge

    for block in range(X // LANES):
        col = column + (block * LANES - (X - 1) / 2.0)

        def one_view(view, sums):
            tile = scal_ref[2, view, block].astype(jnp.int32)
            position = col * scal_ref[0, view, 0] + row_pos * scal_ref[1, view, 0] + centre
            lower = jnp.floor(position)
            weight_low = jnp.maximum(0.0, 1.0 - jnp.abs(position - lower))
            weight_high = jnp.maximum(0.0, 1.0 - jnp.abs(position - (lower + 1.0)))
            weight_low = weight_low.astype(BF16).astype(F32)
            weight_high = weight_high.astype(BF16).astype(F32)
            index = lower.astype(jnp.int32) - (D0 + tile * LANES)
            second = index >= LANES
            index = jnp.bitwise_and(index, LANES - 1)
            offset = pl.multiple_of(tile * LANES, LANES)

            def take(ref, z):
                def part(at_lane):
                    line = jnp.broadcast_to(
                        ref[view, z : z + 1, pl.ds(at_lane, LANES)], (Y, LANES)
                    )
                    return jnp.take_along_axis(line, index, axis=1, mode="promise_in_bounds")

                return jnp.where(second, part(offset + LANES), part(offset))

            return tuple(
                sums[z] + (weight_low * take(low_ref, z) + weight_high * take(high_ref, z))
                for z in range(rows)
            )

        empty = tuple(jnp.zeros((Y, LANES), F32) for _ in range(rows))
        sums = lax.fori_loop(0, views, one_view, empty, unroll=8)
        for z in range(rows):
            done = sums[z] * scale
            ext_ref[z, :, block * LANES : (block + 1) * LANES] = done
            if HALO <= z < rows - HALO:
                own_ref[z - HALO, :, block * LANES : (block + 1) * LANES] = done


def project(data, scale):
    views, rows = data.shape[0], data.shape[1]
    return pl.pallas_call(
        functools.partial(project_kernel, scale),
        out_shape=(
            jax.ShapeDtypeStruct((rows, Y, X), F32),
            jax.ShapeDtypeStruct((rows - 2 * HALO, Y, X), F32),
        ),
        in_specs=[VMEM],
        out_specs=(VMEM, VMEM),
        scratch_shapes=[
            pltpu.VMEM((views, rows, DW), F32),
            pltpu.VMEM((views, rows, DW), F32),
            pltpu.VMEM((3, views, LANES), F32),
            pltpu.SMEM((3, views, LANES), F32),
            pltpu.SemaphoreType.DMA,
        ],
        name="project",
    )(data)


def select_taps(shape, rows_first, dy, column_of):
    param = iota(shape, 0 if rows_first else 1)
    row = iota(shape, 1 if rows_first else 0)
    row = row % BLOCK
    return param, row, column_of(row // 24, (row // 8) % 3, dy)


def first_column(dx, dz, dy):
    return 9 * dz + 3 * dy + dx


def second_column(dx, dz, dy):
    return W_SECOND_AT + (TAPS - 1) - first_column(dx, dz, dy)


def spread(params, column_of, bias):
    channels = params.shape[0]
    height = channels * Y
    high, low = split2(params)
    both = jnp.concatenate([high, low], axis=1)
    rep = (iota((height, channels), 0) // Y == iota((height, channels), 1)).astype(F32)
    rep = rep.astype(BF16)
    shape = (2 * LANES, TILE)
    source = iota(shape, 0)
    col = iota(shape, 1)
    part, inner = col // BLOCK, col % BLOCK
    wanted_half = jnp.where(part == 2, 1, 0)
    usable = (part < 3) & (source // LANES == wanted_half)
    out_col = iota((height, TILE), 1)
    out_inner = out_col % BLOCK
    out_y = iota((height, TILE), 0) % Y
    total = jnp.zeros((height, TILE), F32)
    for dy in range(3):
        wanted = column_of(inner // 24, (inner // 8) % 3, dy)
        pick = usable & (inner < 72) & (source % LANES == wanted)
        if bias and dy == 1:
            pick = pick | (usable & (inner == 72) & (source % LANES == TAPS))
        chosen = dot(both, pick.astype(F32).astype(BF16)).astype(BF16)
        here = (out_inner < 72) & (out_inner % 8 - out_y + 1 == dy)
        if bias and dy == 1:
            here = here | (out_inner == 72)
        total = total + jnp.where(here, dot(rep, chosen), 0.0)
    return total.astype(BF16)


def gather_taps(grad, channels, column_of, bias):
    height = channels * Y
    rep = (iota((channels, height), 1) // Y == iota((channels, height), 0)).astype(F32)
    col = iota((height, BLOCK), 1)
    row_y = iota((height, BLOCK), 0) % Y
    inner = iota((BLOCK, LANES), 0)
    to = iota((BLOCK, LANES), 1)
    total = jnp.zeros((channels, LANES), F32)
    for dy in range(3):
        here = (col < 72) & (col % 8 - row_y + 1 == dy)
        pick = (inner < 72) & (to == column_of(inner // 24, (inner // 8) % 3, dy))
        if bias and dy == 1:
            here = here | (col == 72)
            pick = pick | ((inner == 72) & (to == TAPS))
        summed = jnp.dot(
            rep,
            jnp.where(here, grad, 0.0),
            precision=lax.Precision.HIGHEST,
            preferred_element_type=F32,
        )
        total = total + jnp.dot(
            summed,
            pick.astype(F32),
            precision=lax.Precision.HIGHEST,
            preferred_element_type=F32,
        )
    return total


def shift_columns(value, by):
    if by == 0:
        return value
    rolled = pltpu.roll(value, (-by) % X, 1)
    lane = iota(value.shape, 1)
    return jnp.where(lane == (X - 1 if by > 0 else 0), 0.0, rolled)


def fill_shifted(ref, field):
    for dx in range(3):
        ref[dx] = shift_columns(field, dx - 1)


def patch(ref, slice_index, tile):
    at = pl.multiple_of(slice_index * Y, Y)
    cols = slice(tile * TILE, (tile + 1) * TILE)
    pieces = [ref[dx, pl.ds(at, 3 * Y), cols] for dx in range(3)]
    pieces.append((iota((8, TILE), 0) == 0).astype(F32))
    high, low = split2(jnp.concatenate(pieces, axis=0))
    return high, low


def apply_spread(weights, high, low):
    return dot(weights[:, 0 : 3 * BLOCK], jnp.concatenate([high, low, high], axis=0))


def slice_flag(hidden_slice, hidden_count):
    n_slab = lax.axis_size("slab")
    place = (lax.axis_index("subset") % 2) * n_slab + lax.axis_index("slab")
    outside = ((hidden_slice == 0) & (place == 0)) | (
        (hidden_slice == hidden_count - 1) & (place == 2 * n_slab - 1)
    )
    return jnp.where(outside, 0.0, 1.0).astype(F32)


def forward_kernel(ext_ref, params_ref, pred_ref, first_ref, second_ref, shifted_ref, acc_ref):
    rows = ext_ref.shape[0]
    hidden_count = rows - 2
    params = params_ref[...]
    first = spread(params, first_column, True)
    second = spread(params, second_column, False)
    first_ref[...] = first
    second_ref[...] = second
    second_t = second.astype(F32).T.astype(BF16)
    fill_shifted(shifted_ref, ext_ref[...].reshape(rows * Y, X))
    acc_ref[...] = jnp.zeros(acc_ref.shape, F32)

    def one_slice(hidden_slice, carry):
        flag = slice_flag(hidden_slice, hidden_count)
        at = pl.multiple_of(hidden_slice * Y, Y)
        for tile in range(X // TILE):
            cols = slice(tile * TILE, (tile + 1) * TILE)
            high, low = patch(shifted_ref, hidden_slice, tile)
            hidden = jnp.maximum(apply_spread(first, high, low), 0.0) * flag
            h_high, h_low = split2(hidden)
            main = dot(second_t[BLOCK : 3 * BLOCK], h_high)
            taps = main[0:BLOCK] + main[BLOCK : 2 * BLOCK] + dot(second_t[0:BLOCK], h_low)
            for dx in range(3):
                acc_ref[dx, pl.ds(at, 3 * Y), cols] += taps[24 * dx : 24 * dx + 24]
        return carry

    lax.fori_loop(0, hidden_count, one_slice, 0)
    inner = slice(HALO * Y, (rows - HALO) * Y)
    added = acc_ref[1, inner, :]
    for dx in (0, 2):
        added = added + shift_columns(acc_ref[dx, inner, :], 1 - dx)
    own = ext_ref[HALO : rows - HALO].reshape(added.shape)
    bias = params[0:1, B_SECOND_AT : B_SECOND_AT + 1]
    pred_ref[...] = (own + added + bias).reshape(pred_ref.shape)


def forward(ext, params):
    rows = ext.shape[0]
    height = params.shape[0] * Y
    return pl.pallas_call(
        forward_kernel,
        out_shape=(
            jax.ShapeDtypeStruct((rows - 2 * HALO, Y, X), F32),
            jax.ShapeDtypeStruct((height, TILE), BF16),
            jax.ShapeDtypeStruct((height, TILE), BF16),
        ),
        in_specs=[VMEM, VMEM],
        out_specs=(VMEM, VMEM, VMEM),
        scratch_shapes=[
            pltpu.VMEM((3, rows * Y, X), F32),
            pltpu.VMEM((3, rows * Y, X), F32),
        ],
        cost_estimate=pl.CostEstimate(
            flops=20_000_000_000, bytes_accessed=2_000_000, transcendentals=0
        ),
        name="forward",
    )(ext, params)


def backward_kernel(
    cells,
    ext_ref,
    pred_ref,
    target_ref,
    first_ref,
    second_ref,
    out_ref,
    shifted_ref,
    grad_ref,
    acc1_ref,
    acc2_ref,
):
    rows = ext_ref.shape[0]
    hidden_count = rows - 2
    height = first_ref.shape[0]
    channels = height // Y
    diff = (pred_ref[...] - target_ref[...]).reshape((rows - 2 * HALO) * Y, X)
    resid = 2.0 * diff / cells
    loss = jnp.sum(diff * diff, keepdims=True) / cells
    grad_b2 = jnp.sum(resid, keepdims=True)
    fill_shifted(shifted_ref, ext_ref[...].reshape(rows * Y, X))
    inner = slice(HALO * Y, (rows - HALO) * Y)
    for dx in range(3):
        grad_ref[dx, 0 : HALO * Y, :] = jnp.zeros((HALO * Y, X), F32)
        grad_ref[dx, (rows - HALO) * Y : rows * Y, :] = jnp.zeros((HALO * Y, X), F32)
        grad_ref[dx, inner, :] = shift_columns(resid, dx - 1)
    acc1_ref[...] = jnp.zeros(acc1_ref.shape, F32)
    acc2_ref[...] = jnp.zeros(acc2_ref.shape, F32)
    first = first_ref[...]
    second = second_ref[...]

    def one_slice(hidden_slice, carry):
        flag = slice_flag(hidden_slice, hidden_count)
        sum1 = None
        sum2 = None
        for tile in range(X // TILE):
            high, low = patch(shifted_ref, hidden_slice, tile)
            g_high, g_low = patch(grad_ref, hidden_slice, tile)
            hidden = jnp.maximum(apply_spread(first, high, low), 0.0) * flag
            grad_pre = jnp.where(hidden > 0.0, apply_spread(second, g_high, g_low), 0.0)
            part1 = dot_nt(
                jnp.concatenate(split2(grad_pre), axis=0), jnp.concatenate([high, low], axis=0)
            )
            part2 = dot_nt(
                jnp.concatenate(split2(hidden), axis=0), jnp.concatenate([g_high, g_low], axis=0)
            )
            sum1 = part1 if sum1 is None else sum1 + part1
            sum2 = part2 if sum2 is None else sum2 + part2
        acc1_ref[...] += sum1
        acc2_ref[...] += sum2
        return carry

    lax.fori_loop(0, hidden_count, one_slice, 0)

    def folded(ref):
        value = ref[...]
        value = value[0:height] + value[height : 2 * height]
        return value[:, 0:BLOCK] + value[:, BLOCK : 2 * BLOCK]

    total = gather_taps(folded(acc1_ref), channels, first_column, True)
    total = total + gather_taps(folded(acc2_ref), channels, second_column, False)
    lane = iota(total.shape, 1)
    row = iota(total.shape, 0)
    total = jnp.where((row == 0) & (lane == LOSS_AT), loss, total)
    total = jnp.where((row == 0) & (lane == GRAD_B_SECOND_AT), grad_b2, total)
    out_ref[...] = total


def backward(ext, pred, target, first, second, cells):
    rows = ext.shape[0]
    height = first.shape[0]
    return pl.pallas_call(
        functools.partial(backward_kernel, cells),
        out_shape=jax.ShapeDtypeStruct((height // Y, LANES), F32),
        in_specs=[VMEM] * 5,
        out_specs=VMEM,
        scratch_shapes=[
            pltpu.VMEM((3, rows * Y, X), F32),
            pltpu.VMEM((3, rows * Y, X), F32),
            pltpu.VMEM((2 * height, 2 * BLOCK), F32),
            pltpu.VMEM((2 * height, 2 * BLOCK), F32),
        ],
        name="backward",
    )(ext, pred, target, first, second)


def sum_everywhere(value):
    devices = lax.axis_size("subset") * lax.axis_size("slab")
    apart = 1
    while apart < devices:
        pairs = [(i, i ^ apart) for i in range(devices)]
        value = value + lax.ppermute(value, BOTH, pairs)
        apart *= 2
    return value


def body(sinogram, angles, w_first, b_first, w_second, b_second):
    n_sub = lax.axis_size("subset") // 2
    n_slab = lax.axis_size("slab")
    devices = 2 * n_sub * n_slab
    group = 2 * n_slab
    local_views, z_count = sinogram.shape[0], sinogram.shape[1]
    depth = z_count // group
    channels = w_first.shape[0]
    scale = math.pi / (local_views * group)
    cells = float(n_sub * z_count * Y * X)
    assert devices & (devices - 1) == 0 and channels == 32 and depth >= HALO

    trig = jnp.stack([jnp.cos(angles), jnp.sin(angles)])
    params = jnp.concatenate(
        [
            w_first,
            b_first[:, None],
            jnp.zeros((channels, W_SECOND_AT - TAPS - 1), F32),
            w_second,
            jnp.broadcast_to(b_second, (channels, LANES - W_SECOND_AT - TAPS)),
        ],
        axis=1,
    )
    sent = pack(trig, sinogram, group, depth)
    groups = [list(range(s * group, (s + 1) * group)) for s in range(n_sub)]
    got = lax.all_to_all(sent, BOTH, 0, 0, axis_index_groups=groups)
    got = got.reshape(group * local_views, depth + 2 * HALO, DW)
    ext, own = project(got, scale)

    others = None
    for apart in range(1, n_sub):
        pairs = [(i, (i + apart * group) % devices) for i in range(devices)]
        arrived = lax.ppermute(own, BOTH, pairs)
        others = arrived if others is None else others + arrived
    target = others if n_sub == 2 else others / (n_sub - 1)

    pred, first, second = forward(ext, params)
    partial = backward(ext, pred, target, first, second, cells)
    total = sum_everywhere(partial)
    return (
        pred[None],
        target[None],
        total[0, LOSS_AT],
        total[:, 0:TAPS],
        total[:, TAPS],
        total[:, W_SECOND_AT : W_SECOND_AT + TAPS],
        total[0, GRAD_B_SECOND_AT : GRAD_B_SECOND_AT + 1],
    )


def solution(mesh):
    return jax.shard_map(
        body,
        mesh=mesh,
        in_specs=(P(BOTH, None, None), P(BOTH), P(), P(), P(), P()),
        out_specs=(
            P("subset", "slab", None, None),
            P("subset", "slab", None, None),
            P(),
            P(),
            P(),
            P(),
            P(),
        ),
        check_vma=False,
    )
```

```python
import functools
import math

import jax
import jax.numpy as jnp
from jax import lax
from jax.experimental import pallas as pl
from jax.experimental.pallas import tpu as pltpu
from jax.sharding import PartitionSpec as P

DET = 2048
X = 1024
Y = 8
LANES = 128
TAPS = 27
TILE = 256
BLOCK = 80
W_SECOND_AT = 32
B_SECOND_AT = 59
LOSS_AT = 64
GRAD_B_SECOND_AT = 65
HALO = 2
BOTH = ("subset", "slab")

RADIUS = math.hypot((X - 1) / 2.0, (Y - 1) / 2.0) + 0.25
FIRST_D = math.floor((DET - 1) / 2.0 - RADIUS)
LAST_D = math.floor((DET - 1) / 2.0 + RADIUS) + 1
D0 = FIRST_D // LANES * LANES
DW = -(-(LAST_D + 1 - D0) // LANES) * LANES
assert FIRST_D - D0 >= 6 and D0 + DW <= DET

F32 = jnp.float32
BF16 = jnp.bfloat16
VMEM = pl.BlockSpec(memory_space=pltpu.VMEM)
SMEM = pl.BlockSpec(memory_space=pltpu.SMEM)


def vmem_mib(count):
    return pltpu.CompilerParams(vmem_limit_bytes=count * 2**20)


def iota(shape, dim):
    return lax.broadcasted_iota(jnp.int32, shape, dim)


def split2(value):
    high = value.astype(BF16)
    return high, (value - high.astype(F32)).astype(BF16)


def dot(a, b):
    return jnp.dot(a, b, preferred_element_type=F32)


def dot_nt(a, b):
    return lax.dot_general(a, b, (((1,), (1,)), ((), ())), preferred_element_type=F32)


def pack_kernel(depth, cos_ref, sin_ref, sino_ref, out_ref, rows_ref):
    views, z_count = sino_ref.shape[0], sino_ref.shape[1]
    rows = depth + 2 * HALO
    lane = iota((rows, LANES), 1)
    zeros = jnp.zeros((8, DW), F32)
    for view in range(views):
        rows_ref[0:8, :] = zeros
        rows_ref[8 : 8 + z_count, :] = sino_ref[view, :, D0 : D0 + DW].astype(F32)
        rows_ref[8 + z_count : 16 + z_count, :] = zeros
        head = jnp.zeros((rows, LANES), F32)
        for which, trig_ref in enumerate((cos_ref, sin_ref)):
            left = jnp.full((rows, LANES), trig_ref[view], F32)
            for part in range(3):
                piece = left.astype(BF16).astype(F32)
                left = left - piece
                head = jnp.where(lane == 3 * which + part, piece, head)
        for to in range(out_ref.shape[0]):
            start = 8 + to * depth - HALO
            out_ref[to, view] = rows_ref[start : start + rows, :].astype(BF16)
            first = rows_ref[start : start + rows, 0:LANES]
            out_ref[to, view, :, 0:LANES] = jnp.where(lane < 6, head, first).astype(BF16)


def pack(cosine, sine, sino, group, depth):
    views, z_count = sino.shape[0], sino.shape[1]
    return pl.pallas_call(
        functools.partial(pack_kernel, depth),
        out_shape=jax.ShapeDtypeStruct((group, views, depth + 2 * HALO, DW), BF16),
        in_specs=[SMEM, SMEM, VMEM],
        out_specs=VMEM,
        scratch_shapes=[pltpu.VMEM((z_count + 16, DW), F32)],
        compiler_params=vmem_mib(6),
        name="pack",
    )(cosine, sine, sino)


def project_kernel(scale, data_ref, ext_ref, own_ref, low_ref, high_ref, tab_ref, scal_ref, sem):
    views, rows = data_ref.shape[0], data_ref.shape[1]
    centre = (DET - 1) / 2.0
    head = data_ref[:, 0, 0:LANES].astype(F32)
    cosine = jnp.broadcast_to(head[:, 0:1] + head[:, 1:2] + head[:, 2:3], (views, LANES))
    sine = jnp.broadcast_to(head[:, 3:4] + head[:, 4:5] + head[:, 5:6], (views, LANES))

    def at(col, row):
        return col * cosine + row * sine + centre

    start = (iota((views, LANES), 1) % (X // LANES)).astype(F32) * LANES - (X - 1) / 2.0
    stop = start + (LANES - 1.0)
    edge = (Y - 1) / 2.0
    least = jnp.minimum(
        jnp.minimum(at(start, -edge), at(stop, -edge)), jnp.minimum(at(start, edge), at(stop, edge))
    )
    tab_ref[0] = cosine
    tab_ref[1] = sine
    tab_ref[2] = ((jnp.floor(least).astype(jnp.int32) - D0) // LANES).astype(F32)
    copy = pltpu.make_async_copy(tab_ref, scal_ref, sem)
    copy.start()
    values = data_ref[...].astype(F32)
    low_ref[...] = values
    high_ref[...] = pltpu.roll(values.reshape(views * rows, DW), DW - 1, 1).reshape(values.shape)
    copy.wait()

    lane = iota((views, LANES), 1)
    row_of_lane = (lane // (X // LANES) % Y).astype(F32) - edge
    ends = jnp.floor(at(stop, row_of_lane)) - jnp.floor(at(start, row_of_lane))
    apart = jnp.max(jnp.abs(ends)) >= float(LANES)

    lanes = iota((Y, LANES), 1)
    column = lanes.astype(F32)
    row_pos = iota((Y, LANES), 0).astype(F32) - edge

    def all_blocks(distinct):
        def one_block(block, carry):
            left = block.astype(F32) * LANES - (X - 1) / 2.0
            col = column + left

            def one_view(view, sums):
                tile = scal_ref[2, view, block].astype(jnp.int32)
                cos_part = scal_ref[0, view, 0]
                sin_part = row_pos * scal_ref[1, view, 0]
                position = col * cos_part + sin_part + centre
                lower = jnp.floor(position)
                weight_low = jnp.maximum(0.0, 1.0 - jnp.abs(position - lower))
                weight_high = jnp.maximum(0.0, 1.0 - jnp.abs(position - (lower + 1.0)))
                weight_low = weight_low.astype(BF16).astype(F32)
                weight_high = weight_high.astype(BF16).astype(F32)
                base = D0 + tile * LANES
                index = lower.astype(jnp.int32) - base
                second = index >= LANES
                index = jnp.bitwise_and(index, LANES - 1)
                offset = pl.multiple_of(tile * LANES, LANES)
                if distinct:
                    end1 = left * cos_part + sin_part + centre
                    end2 = (left + (LANES - 1.0)) * cos_part + sin_part + centre
                    least_index = jnp.floor(jnp.minimum(end1, end2)).astype(jnp.int32) - base
                    in_first = lanes >= least_index

                def take(ref, z):
                    def line(at_lane):
                        return jnp.broadcast_to(
                            ref[view, z : z + 1, pl.ds(at_lane, LANES)], (Y, LANES)
                        )

                    def pick(values):
                        return jnp.take_along_axis(
                            values, index, axis=1, mode="promise_in_bounds"
                        )

                    one, two = line(offset), line(offset + LANES)
                    if distinct:
                        return pick(jnp.where(in_first, one, two))
                    return jnp.where(second, pick(two), pick(one))

                return tuple(
                    sums[z] + (weight_low * take(low_ref, z) + weight_high * take(high_ref, z))
                    for z in range(rows)
                )

            empty = tuple(jnp.zeros((Y, LANES), F32) for _ in range(rows))
            sums = lax.fori_loop(0, views, one_view, empty, unroll=16 if distinct else 1)
            cols = pl.ds(pl.multiple_of(block * LANES, LANES), LANES)
            for z in range(rows):
                done = sums[z] * scale
                ext_ref[z, :, cols] = done
                if HALO <= z < rows - HALO:
                    own_ref[z - HALO, :, cols] = done
            return carry

        lax.fori_loop(0, X // LANES, one_block, 0)

    pl.when(apart)(lambda: all_blocks(False))
    pl.when(jnp.logical_not(apart))(lambda: all_blocks(True))


def project(data, scale):
    views, rows = data.shape[0], data.shape[1]
    return pl.pallas_call(
        functools.partial(project_kernel, scale),
        out_shape=(
            jax.ShapeDtypeStruct((rows, Y, X), F32),
            jax.ShapeDtypeStruct((rows - 2 * HALO, Y, X), F32),
        ),
        in_specs=[VMEM],
        out_specs=(VMEM, VMEM),
        scratch_shapes=[
            pltpu.VMEM((views, rows, DW), F32),
            pltpu.VMEM((views, rows, DW), F32),
            pltpu.VMEM((3, views, LANES), F32),
            pltpu.SMEM((3, views, LANES), F32),
            pltpu.SemaphoreType.DMA,
        ],
        compiler_params=vmem_mib(14),
        name="project",
    )(data)


def select_taps(shape, rows_first, dy, column_of):
    param = iota(shape, 0 if rows_first else 1)
    row = iota(shape, 1 if rows_first else 0)
    row = row % BLOCK
    return param, row, column_of(row // 24, (row // 8) % 3, dy)


def first_column(dx, dz, dy):
    return 9 * dz + 3 * dy + dx


def second_column(dx, dz, dy):
    return W_SECOND_AT + (TAPS - 1) - first_column(dx, dz, dy)


def spread(params, column_of, bias):
    channels = params.shape[0]
    height = channels * Y
    high, low = split2(params)
    both = jnp.concatenate([high, low], axis=1)
    rep = (iota((height, channels), 0) // Y == iota((height, channels), 1)).astype(F32)
    rep = rep.astype(BF16)
    shape = (2 * LANES, TILE)
    source = iota(shape, 0)
    col = iota(shape, 1)
    part, inner = col // BLOCK, col % BLOCK
    wanted_half = jnp.where(part == 2, 1, 0)
    usable = (part < 3) & (source // LANES == wanted_half)
    out_col = iota((height, TILE), 1)
    out_inner = out_col % BLOCK
    out_y = iota((height, TILE), 0) % Y
    total = jnp.zeros((height, TILE), F32)
    for dy in range(3):
        wanted = column_of(inner // 24, (inner // 8) % 3, dy)
        pick = usable & (inner < 72) & (source % LANES == wanted)
        if bias and dy == 1:
            pick = pick | (usable & (inner == 72) & (source % LANES == TAPS))
        chosen = dot(both, pick.astype(F32).astype(BF16)).astype(BF16)
        here = (out_inner < 72) & (out_inner % 8 - out_y + 1 == dy)
        if bias and dy == 1:
            here = here | (out_inner == 72)
        total = total + jnp.where(here, dot(rep, chosen), 0.0)
    return total.astype(BF16)


def gather_taps(grad, channels, column_of, bias):
    height = channels * Y
    rep = (iota((channels, height), 1) // Y == iota((channels, height), 0)).astype(F32)
    col = iota((height, BLOCK), 1)
    row_y = iota((height, BLOCK), 0) % Y
    inner = iota((BLOCK, LANES), 0)
    to = iota((BLOCK, LANES), 1)
    total = jnp.zeros((channels, LANES), F32)
    for dy in range(3):
        here = (col < 72) & (col % 8 - row_y + 1 == dy)
        pick = (inner < 72) & (to == column_of(inner // 24, (inner // 8) % 3, dy))
        if bias and dy == 1:
            here = here | (col == 72)
            pick = pick | ((inner == 72) & (to == TAPS))
        summed = jnp.dot(
            rep,
            jnp.where(here, grad, 0.0),
            precision=lax.Precision.HIGHEST,
            preferred_element_type=F32,
        )
        total = total + jnp.dot(
            summed,
            pick.astype(F32),
            precision=lax.Precision.HIGHEST,
            preferred_element_type=F32,
        )
    return total


def shift_columns(value, by):
    if by == 0:
        return value
    rolled = pltpu.roll(value, (-by) % X, 1)
    lane = iota(value.shape, 1)
    return jnp.where(lane == (X - 1 if by > 0 else 0), 0.0, rolled)


def fill_shifted(ref, field):
    for dx in range(3):
        ref[dx] = shift_columns(field, dx - 1)


def patch(ref, slice_index, tile):
    at = pl.multiple_of(slice_index * Y, Y)
    cols = slice(tile * TILE, (tile + 1) * TILE)
    pieces = [ref[dx, pl.ds(at, 3 * Y), cols] for dx in range(3)]
    pieces.append((iota((8, TILE), 0) == 0).astype(F32))
    high, low = split2(jnp.concatenate(pieces, axis=0))
    return high, low


def apply_spread(weights, high, low):
    return dot(weights[:, 0 : 3 * BLOCK], jnp.concatenate([high, low, high], axis=0))


def slice_flag(hidden_slice, hidden_count):
    n_slab = lax.axis_size("slab")
    place = (lax.axis_index("subset") % 2) * n_slab + lax.axis_index("slab")
    outside = ((hidden_slice == 0) & (place == 0)) | (
        (hidden_slice == hidden_count - 1) & (place == 2 * n_slab - 1)
    )
    return jnp.where(outside, 0.0, 1.0).astype(F32)


def forward_kernel(ext_ref, params_ref, pred_ref, first_ref, second_ref, shifted_ref, acc_ref):
    rows = ext_ref.shape[0]
    hidden_count = rows - 2
    params = params_ref[...]
    first = spread(params, first_column, True)
    second = spread(params, second_column, False)
    first_ref[...] = first
    second_ref[...] = second
    second_t = second.astype(F32).T.astype(BF16)
    fill_shifted(shifted_ref, ext_ref[...].reshape(rows * Y, X))
    acc_ref[...] = jnp.zeros(acc_ref.shape, F32)

    def one_slice(hidden_slice, carry):
        flag = slice_flag(hidden_slice, hidden_count)
        at = pl.multiple_of(hidden_slice * Y, Y)
        for tile in range(X // TILE):
            cols = slice(tile * TILE, (tile + 1) * TILE)
            high, low = patch(shifted_ref, hidden_slice, tile)
            hidden = jnp.maximum(apply_spread(first, high, low), 0.0) * flag
            h_high, h_low = split2(hidden)
            main = dot(second_t[BLOCK : 3 * BLOCK], h_high)
            taps = main[0:BLOCK] + main[BLOCK : 2 * BLOCK] + dot(second_t[0:BLOCK], h_low)
            for dx in range(3):
                acc_ref[dx, pl.ds(at, 3 * Y), cols] += taps[24 * dx : 24 * dx + 24]
        return carry

    lax.fori_loop(0, hidden_count, one_slice, 0)
    inner = slice(HALO * Y, (rows - HALO) * Y)
    added = acc_ref[1, inner, :]
    for dx in (0, 2):
        added = added + shift_columns(acc_ref[dx, inner, :], 1 - dx)
    own = ext_ref[HALO : rows - HALO].reshape(added.shape)
    bias = params[0:1, B_SECOND_AT : B_SECOND_AT + 1]
    pred_ref[...] = (own + added + bias).reshape(pred_ref.shape)


def forward(ext, params):
    rows = ext.shape[0]
    height = params.shape[0] * Y
    return pl.pallas_call(
        forward_kernel,
        out_shape=(
            jax.ShapeDtypeStruct((rows - 2 * HALO, Y, X), F32),
            jax.ShapeDtypeStruct((height, TILE), BF16),
            jax.ShapeDtypeStruct((height, TILE), BF16),
        ),
        in_specs=[VMEM, VMEM],
        out_specs=(VMEM, VMEM, VMEM),
        scratch_shapes=[
            pltpu.VMEM((3, rows * Y, X), F32),
            pltpu.VMEM((3, rows * Y, X), F32),
        ],
        cost_estimate=pl.CostEstimate(
            flops=20_000_000_000, bytes_accessed=2_000_000, transcendentals=0
        ),
        compiler_params=vmem_mib(14),
        name="forward",
    )(ext, params)


def backward_kernel(
    cells,
    ext_ref,
    pred_ref,
    target_ref,
    first_ref,
    second_ref,
    out_ref,
    shifted_ref,
    grad_ref,
    acc1_ref,
    acc2_ref,
):
    rows = ext_ref.shape[0]
    hidden_count = rows - 2
    height = first_ref.shape[0]
    channels = height // Y
    diff = (pred_ref[...] - target_ref[...]).reshape((rows - 2 * HALO) * Y, X)
    resid = 2.0 * diff / cells
    loss = jnp.sum(diff * diff, keepdims=True) / cells
    grad_b2 = jnp.sum(resid, keepdims=True)
    fill_shifted(shifted_ref, ext_ref[...].reshape(rows * Y, X))
    inner = slice(HALO * Y, (rows - HALO) * Y)
    for dx in range(3):
        grad_ref[dx, 0 : HALO * Y, :] = jnp.zeros((HALO * Y, X), F32)
        grad_ref[dx, (rows - HALO) * Y : rows * Y, :] = jnp.zeros((HALO * Y, X), F32)
        grad_ref[dx, inner, :] = shift_columns(resid, dx - 1)
    acc1_ref[...] = jnp.zeros(acc1_ref.shape, F32)
    acc2_ref[...] = jnp.zeros(acc2_ref.shape, F32)
    first = first_ref[...]
    second = second_ref[...]

    def one_slice(hidden_slice, carry):
        flag = slice_flag(hidden_slice, hidden_count)
        sum1 = None
        sum2 = None
        for tile in range(X // TILE):
            high, low = patch(shifted_ref, hidden_slice, tile)
            g_high, g_low = patch(grad_ref, hidden_slice, tile)
            hidden = jnp.maximum(apply_spread(first, high, low), 0.0) * flag
            grad_pre = jnp.where(hidden > 0.0, apply_spread(second, g_high, g_low), 0.0)
            part1 = dot_nt(
                jnp.concatenate(split2(grad_pre), axis=0), jnp.concatenate([high, low], axis=0)
            )
            part2 = dot_nt(
                jnp.concatenate(split2(hidden), axis=0), jnp.concatenate([g_high, g_low], axis=0)
            )
            sum1 = part1 if sum1 is None else sum1 + part1
            sum2 = part2 if sum2 is None else sum2 + part2
        acc1_ref[...] += sum1
        acc2_ref[...] += sum2
        return carry

    lax.fori_loop(0, hidden_count, one_slice, 0)

    def folded(ref):
        value = ref[...]
        value = value[0:height] + value[height : 2 * height]
        return value[:, 0:BLOCK] + value[:, BLOCK : 2 * BLOCK]

    total = gather_taps(folded(acc1_ref), channels, first_column, True)
    total = total + gather_taps(folded(acc2_ref), channels, second_column, False)
    lane = iota((channels, LANES), 1)
    diagonal = lane == iota((channels, LANES), 0)
    line = jnp.sum(jnp.where(diagonal, total[:, TAPS : TAPS + 1], 0.0), axis=0, keepdims=True)
    line = jnp.where(lane[0:8] == LOSS_AT, loss, jnp.broadcast_to(line, (8, LANES)))
    out_ref[0:channels, :] = total
    out_ref[channels : channels + 8, :] = jnp.where(lane[0:8] == GRAD_B_SECOND_AT, grad_b2, line)


def backward(ext, pred, target, first, second, cells):
    rows = ext.shape[0]
    height = first.shape[0]
    return pl.pallas_call(
        functools.partial(backward_kernel, cells),
        out_shape=jax.ShapeDtypeStruct((height // Y + 8, LANES), F32),
        in_specs=[VMEM] * 5,
        out_specs=VMEM,
        scratch_shapes=[
            pltpu.VMEM((3, rows * Y, X), F32),
            pltpu.VMEM((3, rows * Y, X), F32),
            pltpu.VMEM((2 * height, 2 * BLOCK), F32),
            pltpu.VMEM((2 * height, 2 * BLOCK), F32),
        ],
        compiler_params=vmem_mib(20),
        name="backward",
    )(ext, pred, target, first, second)


def finish_kernel(one_ref, two_ref, loss_ref, w1_ref, b1_ref, w2_ref, b2_ref):
    total = one_ref[...] + two_ref[...]
    channels = w1_ref.shape[0]
    line = total[channels : channels + 1]
    loss_ref[...] = line[:, LOSS_AT : LOSS_AT + 1]
    w1_ref[...] = total[0:channels, 0:TAPS]
    b1_ref[...] = line[:, 0:channels]
    w2_ref[...] = total[0:channels, W_SECOND_AT : W_SECOND_AT + TAPS]
    b2_ref[...] = line[:, GRAD_B_SECOND_AT : GRAD_B_SECOND_AT + 1]


def sum_everywhere(value, channels):
    devices = lax.axis_size("subset") * lax.axis_size("slab")
    apart = 1
    while True:
        arrived = lax.ppermute(value, BOTH, [(i, i ^ apart) for i in range(devices)])
        apart *= 2
        if apart == devices:
            break
        value = value + arrived
    shapes = ((1, 1), (channels, TAPS), (1, channels), (channels, TAPS), (1, 1))
    return pl.pallas_call(
        finish_kernel,
        out_shape=tuple(jax.ShapeDtypeStruct(shape, F32) for shape in shapes),
        in_specs=[VMEM, VMEM],
        out_specs=(VMEM,) * 5,
        compiler_params=vmem_mib(1),
        name="finish",
    )(value, arrived)


def body(sinogram, angles, w_first, b_first, w_second, b_second):
    n_sub = lax.axis_size("subset") // 2
    n_slab = lax.axis_size("slab")
    devices = 2 * n_sub * n_slab
    group = 2 * n_slab
    local_views, z_count = sinogram.shape[0], sinogram.shape[1]
    depth = z_count // group
    channels = w_first.shape[0]
    scale = math.pi / (local_views * group)
    cells = float(n_sub * z_count * Y * X)
    assert devices & (devices - 1) == 0 and channels == 32 and depth >= HALO

    params = jnp.concatenate(
        [
            w_first,
            b_first[:, None],
            jnp.zeros((channels, W_SECOND_AT - TAPS - 1), F32),
            w_second,
            jnp.broadcast_to(b_second, (channels, LANES - W_SECOND_AT - TAPS)),
        ],
        axis=1,
    )
    sent = pack(jnp.cos(angles), jnp.sin(angles), sinogram, group, depth)
    groups = [list(range(s * group, (s + 1) * group)) for s in range(n_sub)]
    got = lax.all_to_all(sent, BOTH, 0, 0, axis_index_groups=groups)
    got = got.reshape(group * local_views, depth + 2 * HALO, DW)
    ext, own = project(got, scale)

    others = None
    for apart in range(1, n_sub):
        pairs = [(i, (i + apart * group) % devices) for i in range(devices)]
        arrived = lax.ppermute(own, BOTH, pairs)
        others = arrived if others is None else others + arrived
    target = others if n_sub == 2 else others / (n_sub - 1)

    pred, first, second = forward(ext, params)
    partial = backward(ext, pred, target, first, second, cells)
    loss, grad_w1, grad_b1, grad_w2, grad_b2 = sum_everywhere(partial, channels)
    return (
        pred[None],
        target[None],
        loss.reshape(()),
        grad_w1,
        grad_b1.reshape(-1),
        grad_w2,
        grad_b2.reshape(-1),
    )


def solution(mesh):
    return jax.shard_map(
        body,
        mesh=mesh,
        in_specs=(P(BOTH, None, None), P(BOTH), P(), P(), P(), P()),
        out_specs=(
            P("subset", "slab", None, None),
            P("subset", "slab", None, None),
            P(),
            P(),
            P(),
            P(),
            P(),
        ),
        check_vma=False,
    )
```

```python
import functools
import math

import jax
import jax.numpy as jnp
from jax import lax
from jax.experimental import pallas as pl
from jax.experimental.pallas import tpu as pltpu
from jax.sharding import PartitionSpec as P

DET = 2048
X = 1024
Y = 8
LANES = 128
TAPS = 27
TILE = 256
BLOCK = 80
W_SECOND_AT = 32
B_SECOND_AT = 59
LOSS_AT = 64
GRAD_B_SECOND_AT = 65
HALO = 2
BOTH = ("subset", "slab")

RADIUS = math.hypot((X - 1) / 2.0, (Y - 1) / 2.0) + 0.25
FIRST_D = math.floor((DET - 1) / 2.0 - RADIUS)
LAST_D = math.floor((DET - 1) / 2.0 + RADIUS) + 1
D0 = FIRST_D // LANES * LANES
DW = -(-(LAST_D + 1 - D0) // LANES) * LANES
assert FIRST_D - D0 >= 6 and D0 + DW <= DET

F32 = jnp.float32
BF16 = jnp.bfloat16
VMEM = pl.BlockSpec(memory_space=pltpu.VMEM)
SMEM = pl.BlockSpec(memory_space=pltpu.SMEM)


def vmem_mib(count):
    return pltpu.CompilerParams(vmem_limit_bytes=count * 2**20)


def iota(shape, dim):
    return lax.broadcasted_iota(jnp.int32, shape, dim)


def split2(value):
    high = value.astype(BF16)
    return high, (value - high.astype(F32)).astype(BF16)


def dot(a, b):
    return jnp.dot(a, b, preferred_element_type=F32)


def dot_nt(a, b):
    return lax.dot_general(a, b, (((1,), (1,)), ((), ())), preferred_element_type=F32)


def pack_kernel(depth, angle_ref, sino_ref, out_ref, held_ref, rows_ref, sems):
    views, z_count = sino_ref.shape[0], sino_ref.shape[1]
    rows = depth + 2 * HALO
    copies = [
        pltpu.make_async_copy(
            sino_ref.at[view, :, pl.ds(D0, DW)], held_ref.at[view], sems.at[view]
        )
        for view in range(views)
    ]
    for copy in copies:
        copy.start()
    lane = iota((rows, LANES), 1)
    zeros = jnp.zeros((8, DW), F32)
    rows_ref[0:8, :] = zeros
    rows_ref[8 + z_count : 16 + z_count, :] = zeros
    for view in range(views):
        angle = jnp.full((rows, LANES), angle_ref[view], F32)
        head = jnp.zeros((rows, LANES), F32)
        for which, left in enumerate((jnp.cos(angle), jnp.sin(angle))):
            for part in range(3):
                piece = left.astype(BF16).astype(F32)
                left = left - piece
                head = jnp.where(lane == 3 * which + part, piece, head)
        copies[view].wait()
        rows_ref[8 : 8 + z_count, :] = held_ref[view].astype(F32)
        for to in range(out_ref.shape[0]):
            start = 8 + to * depth - HALO
            out_ref[to, view] = rows_ref[start : start + rows, :].astype(BF16)
            first = rows_ref[start : start + rows, 0:LANES]
            out_ref[to, view, :, 0:LANES] = jnp.where(lane < 6, head, first).astype(BF16)


def pack(angles, sino, group, depth):
    views, z_count = sino.shape[0], sino.shape[1]
    return pl.pallas_call(
        functools.partial(pack_kernel, depth),
        out_shape=jax.ShapeDtypeStruct((group, views, depth + 2 * HALO, DW), BF16),
        in_specs=[SMEM, pl.BlockSpec(memory_space=pltpu.HBM)],
        out_specs=VMEM,
        scratch_shapes=[
            pltpu.VMEM((views, z_count, DW), BF16),
            pltpu.VMEM((z_count + 16, DW), F32),
            pltpu.SemaphoreType.DMA((views,)),
        ],
        name="pack",
    )(angles, sino)


def project_kernel(scale, data_ref, ext_ref, own_ref, low_ref, high_ref, tab_ref, scal_ref, sem):
    views, rows = data_ref.shape[0], data_ref.shape[1]
    centre = (DET - 1) / 2.0
    head = data_ref[:, 0, 0:LANES].astype(F32)
    cosine = jnp.broadcast_to(head[:, 0:1] + head[:, 1:2] + head[:, 2:3], (views, LANES))
    sine = jnp.broadcast_to(head[:, 3:4] + head[:, 4:5] + head[:, 5:6], (views, LANES))

    def at(col, row):
        return col * cosine + row * sine + centre

    start = (iota((views, LANES), 1) % (X // LANES)).astype(F32) * LANES - (X - 1) / 2.0
    stop = start + (LANES - 1.0)
    edge = (Y - 1) / 2.0
    least = jnp.minimum(
        jnp.minimum(at(start, -edge), at(stop, -edge)), jnp.minimum(at(start, edge), at(stop, edge))
    )
    tab_ref[0] = cosine
    tab_ref[1] = sine
    tab_ref[2] = ((jnp.floor(least).astype(jnp.int32) - D0) // LANES).astype(F32)
    copy = pltpu.make_async_copy(tab_ref, scal_ref, sem)
    copy.start()
    values = data_ref[...].astype(F32)
    moved = pltpu.roll(values.reshape(views * rows, DW), DW - 1, 1).reshape(values.shape)
    for tile in range(DW // LANES):
        cols = slice(tile * LANES, (tile + 1) * LANES)
        low_ref[:, tile] = values[:, :, cols]
        high_ref[:, tile] = moved[:, :, cols]
    copy.wait()

    lane = iota((views, LANES), 1)
    row_of_lane = (lane // (X // LANES) % Y).astype(F32) - edge
    ends = jnp.floor(at(stop, row_of_lane)) - jnp.floor(at(start, row_of_lane))
    apart = jnp.max(jnp.abs(ends)) >= float(LANES)

    lanes = iota((Y, LANES), 1)
    column = lanes.astype(F32)
    row_pos = iota((Y, LANES), 0).astype(F32) - edge

    def all_blocks(distinct):
        def one_block(block, carry):
            left = block.astype(F32) * LANES - (X - 1) / 2.0
            col = column + left

            def one_view(view, sums):
                tile = scal_ref[2, view, block].astype(jnp.int32)
                cos_part = scal_ref[0, view, 0]
                sin_part = row_pos * scal_ref[1, view, 0]
                position = col * cos_part + sin_part + centre
                lower = jnp.floor(position)
                weight_low = jnp.maximum(0.0, 1.0 - jnp.abs(position - lower))
                weight_high = jnp.maximum(0.0, 1.0 - jnp.abs(position - (lower + 1.0)))
                weight_low = weight_low.astype(BF16).astype(F32)
                weight_high = weight_high.astype(BF16).astype(F32)
                base = D0 + tile * LANES
                index = lower.astype(jnp.int32) - base
                second = index >= LANES
                index = jnp.bitwise_and(index, LANES - 1)
                if distinct:
                    end1 = left * cos_part + sin_part + centre
                    end2 = (left + (LANES - 1.0)) * cos_part + sin_part + centre
                    least_index = jnp.floor(jnp.minimum(end1, end2)).astype(jnp.int32) - base
                    in_first = lanes >= least_index

                def take(ref, z):
                    def line(at_tile):
                        return ref[view, at_tile, pl.ds(z, Y, stride=0), :]

                    def pick(values):
                        return jnp.take_along_axis(
                            values, index, axis=1, mode="promise_in_bounds"
                        )

                    one, two = line(tile), line(tile + 1)
                    if distinct:
                        return pick(jnp.where(in_first, one, two))
                    return jnp.where(second, pick(two), pick(one))

                return tuple(
                    sums[z] + (weight_low * take(low_ref, z) + weight_high * take(high_ref, z))
                    for z in range(rows)
                )

            empty = tuple(jnp.zeros((Y, LANES), F32) for _ in range(rows))
            sums = lax.fori_loop(0, views, one_view, empty, unroll=16 if distinct else 1)
            cols = pl.ds(pl.multiple_of(block * LANES, LANES), LANES)
            for z in range(rows):
                done = sums[z] * scale
                ext_ref[z, :, cols] = done
                if HALO <= z < rows - HALO:
                    own_ref[z - HALO, :, cols] = done
            return carry

        lax.fori_loop(0, X // LANES, one_block, 0)

    pl.when(apart)(lambda: all_blocks(False))
    pl.when(jnp.logical_not(apart))(lambda: all_blocks(True))


def project(data, scale):
    views, rows = data.shape[0], data.shape[1]
    return pl.pallas_call(
        functools.partial(project_kernel, scale),
        out_shape=(
            jax.ShapeDtypeStruct((rows, Y, X), F32),
            jax.ShapeDtypeStruct((rows - 2 * HALO, Y, X), F32),
        ),
        in_specs=[VMEM],
        out_specs=(VMEM, VMEM),
        scratch_shapes=[
            pltpu.VMEM((views, DW // LANES, rows, LANES), F32),
            pltpu.VMEM((views, DW // LANES, rows, LANES), F32),
            pltpu.VMEM((3, views, LANES), F32),
            pltpu.SMEM((3, views, LANES), F32),
            pltpu.SemaphoreType.DMA,
        ],
        compiler_params=vmem_mib(14),
        name="project",
    )(data)


def select_taps(shape, rows_first, dy, column_of):
    param = iota(shape, 0 if rows_first else 1)
    row = iota(shape, 1 if rows_first else 0)
    row = row % BLOCK
    return param, row, column_of(row // 24, (row // 8) % 3, dy)


def first_column(dx, dz, dy):
    return 9 * dz + 3 * dy + dx


def second_column(dx, dz, dy):
    return W_SECOND_AT + (TAPS - 1) - first_column(dx, dz, dy)


def spread(params, column_of, bias):
    channels = params.shape[0]
    height = channels * Y
    high, low = split2(params)
    both = jnp.concatenate([high, low], axis=1)
    rep = (iota((height, channels), 0) // Y == iota((height, channels), 1)).astype(F32)
    rep = rep.astype(BF16)
    shape = (2 * LANES, TILE)
    source = iota(shape, 0)
    col = iota(shape, 1)
    part, inner = col // BLOCK, col % BLOCK
    wanted_half = jnp.where(part == 2, 1, 0)
    usable = (part < 3) & (source // LANES == wanted_half)
    out_col = iota((height, TILE), 1)
    out_inner = out_col % BLOCK
    out_y = iota((height, TILE), 0) % Y
    total = jnp.zeros((height, TILE), F32)
    for dy in range(3):
        wanted = column_of(inner // 24, (inner // 8) % 3, dy)
        pick = usable & (inner < 72) & (source % LANES == wanted)
        if bias and dy == 1:
            pick = pick | (usable & (inner == 72) & (source % LANES == TAPS))
        chosen = dot(both, pick.astype(F32).astype(BF16)).astype(BF16)
        here = (out_inner < 72) & (out_inner % 8 - out_y + 1 == dy)
        if bias and dy == 1:
            here = here | (out_inner == 72)
        total = total + jnp.where(here, dot(rep, chosen), 0.0)
    return total.astype(BF16)


def gather_taps(grads, channels):
    height = channels * Y
    col = iota((height, LANES), 1)
    row_y = iota((height, LANES), 0) % Y
    inner = iota((LANES, LANES), 0)
    to = iota((LANES, LANES), 1)
    pieces = []
    picks = []
    for grad, column_of, bias in grads:
        for dy in range(3):
            here = (col < 72) & (col % 8 - row_y + 1 == dy)
            pick = (inner < 72) & (to == column_of(inner // 24, (inner // 8) % 3, dy))
            if bias and dy == 1:
                here = here | (col == 72)
                pick = pick | ((inner == 72) & (to == TAPS))
            masked = jnp.where(here, grad, 0.0).reshape(channels, Y, LANES)
            pieces.append(jnp.sum(masked, axis=1))
            picks.append(pick.astype(F32))
    return jnp.dot(
        jnp.concatenate(pieces, axis=1),
        jnp.concatenate(picks, axis=0),
        precision=lax.Precision.HIGHEST,
        preferred_element_type=F32,
    )


def shift_columns(value, by):
    if by == 0:
        return value
    rolled = pltpu.roll(value, (-by) % X, 1)
    lane = iota(value.shape, 1)
    return jnp.where(lane == (X - 1 if by > 0 else 0), 0.0, rolled)


def fill_shifted(ref, field):
    for dx in range(3):
        ref[dx] = shift_columns(field, dx - 1)


def patch(ref, slice_index, tile):
    at = pl.multiple_of(slice_index * Y, Y)
    cols = slice(tile * TILE, (tile + 1) * TILE)
    pieces = [ref[dx, pl.ds(at, 3 * Y), cols] for dx in range(3)]
    pieces.append((iota((8, TILE), 0) == 0).astype(F32))
    high, low = split2(jnp.concatenate(pieces, axis=0))
    return high, low


def apply_spread(weights, high, low):
    return dot(weights[:, 0 : 3 * BLOCK], jnp.concatenate([high, low, high], axis=0))


def slice_flag(hidden_slice, hidden_count):
    n_slab = lax.axis_size("slab")
    place = (lax.axis_index("subset") % 2) * n_slab + lax.axis_index("slab")
    outside = ((hidden_slice == 0) & (place == 0)) | (
        (hidden_slice == hidden_count - 1) & (place == 2 * n_slab - 1)
    )
    return jnp.where(outside, 0.0, 1.0).astype(F32)


def weights_kernel(params_ref, first_ref, second_ref, turned_ref):
    params = params_ref[...]
    second = spread(params, second_column, False)
    first_ref[...] = spread(params, first_column, True)
    second_ref[...] = second
    turned_ref[...] = second.astype(F32).T.astype(BF16)


def weights(params):
    height = params.shape[0] * Y
    return pl.pallas_call(
        weights_kernel,
        out_shape=(
            jax.ShapeDtypeStruct((height, TILE), BF16),
            jax.ShapeDtypeStruct((height, TILE), BF16),
            jax.ShapeDtypeStruct((TILE, height), BF16),
        ),
        in_specs=[VMEM],
        out_specs=(VMEM,) * 3,
        compiler_params=vmem_mib(8),
        name="weights",
    )(params)


def forward_kernel(
    ext_ref, params_ref, first_ref, turned_ref, pred_ref, again_ref, shifted_ref, hidden_ref, acc_ref
):
    rows = ext_ref.shape[0]
    hidden_count = rows - 2
    height = first_ref.shape[0]
    first = first_ref[...]
    fill_shifted(shifted_ref, ext_ref[...].reshape(rows * Y, X))
    acc_ref[...] = jnp.zeros(acc_ref.shape, F32)

    def one_slice(hidden_slice, carry):
        flag = slice_flag(hidden_slice, hidden_count)
        at = pl.multiple_of(hidden_slice * Y, Y)
        kept = pl.ds(pl.multiple_of(hidden_slice * height, height), height)
        for tile in range(X // TILE):
            cols = slice(tile * TILE, (tile + 1) * TILE)
            high, low = patch(shifted_ref, hidden_slice, tile)
            hidden = jnp.maximum(apply_spread(first, high, low), 0.0) * flag
            h_high, h_low = split2(hidden)
            hidden_ref[kept, cols] = h_high
            main = dot(turned_ref[BLOCK : 3 * BLOCK], h_high)
            taps = main[0:BLOCK] + main[BLOCK : 2 * BLOCK] + dot(turned_ref[0:BLOCK], h_low)
            for dx in range(3):
                acc_ref[dx, pl.ds(at, 3 * Y), cols] += taps[24 * dx : 24 * dx + 24]
        return carry

    lax.fori_loop(0, hidden_count, one_slice, 0)
    inner = slice(HALO * Y, (rows - HALO) * Y)
    added = acc_ref[1, inner, :]
    for dx in (0, 2):
        added = added + shift_columns(acc_ref[dx, inner, :], 1 - dx)
    own = ext_ref[HALO : rows - HALO].reshape(added.shape)
    bias = params_ref[0:1, B_SECOND_AT : B_SECOND_AT + 1]
    pred = (own + added + bias).reshape(pred_ref.shape)
    pred_ref[...] = pred
    again_ref[...] = pred


def forward(ext, params, first, turned):
    rows = ext.shape[0]
    height = first.shape[0]
    own = jax.ShapeDtypeStruct((rows - 2 * HALO, Y, X), F32)
    return pl.pallas_call(
        forward_kernel,
        out_shape=(
            own,
            own,
            jax.ShapeDtypeStruct((3, rows * Y, X), F32),
            jax.ShapeDtypeStruct(((rows - 2) * height, X), BF16),
        ),
        in_specs=[VMEM] * 4,
        out_specs=(VMEM,) * 4,
        scratch_shapes=[pltpu.VMEM((3, rows * Y, X), F32)],
        cost_estimate=pl.CostEstimate(
            flops=20_000_000_000, bytes_accessed=2_000_000, transcendentals=0
        ),
        compiler_params=vmem_mib(18),
        name="forward",
    )(ext, params, first, turned)


def padded_rows(high, low):
    none = jnp.zeros((LANES - BLOCK, high.shape[1]), BF16)
    return jnp.concatenate([high, none, low, none], axis=0)


def backward_kernel(
    cells,
    shifted_ref,
    hidden_ref,
    pred_ref,
    target_ref,
    second_ref,
    out_ref,
    target_out_ref,
    grad_ref,
    acc1_ref,
    acc2_ref,
):
    rows = shifted_ref.shape[1] // Y
    hidden_count = rows - 2
    height = second_ref.shape[0]
    channels = height // Y
    target = target_ref[...]
    target_out_ref[...] = target
    diff = (pred_ref[...] - target).reshape((rows - 2 * HALO) * Y, X)
    resid = 2.0 * diff / cells
    loss = jnp.sum(diff * diff, keepdims=True) / cells
    grad_b2 = jnp.sum(resid, keepdims=True)
    inner = slice(HALO * Y, (rows - HALO) * Y)
    for dx in range(3):
        grad_ref[dx, 0 : HALO * Y, :] = jnp.zeros((HALO * Y, X), F32)
        grad_ref[dx, (rows - HALO) * Y : rows * Y, :] = jnp.zeros((HALO * Y, X), F32)
        grad_ref[dx, inner, :] = shift_columns(resid, dx - 1)
    acc1_ref[...] = jnp.zeros(acc1_ref.shape, F32)
    acc2_ref[...] = jnp.zeros(acc2_ref.shape, F32)
    second = second_ref[...]

    def one_slice(hidden_slice, carry):
        kept = pl.ds(pl.multiple_of(hidden_slice * height, height), height)
        sum1 = None
        sum2 = None
        for tile in range(X // TILE):
            cols = slice(tile * TILE, (tile + 1) * TILE)
            high, low = patch(shifted_ref, hidden_slice, tile)
            g_high, g_low = patch(grad_ref, hidden_slice, tile)
            hidden = hidden_ref[kept, cols]
            grad_hidden = apply_spread(second, g_high, g_low)
            grad_pre = jnp.where(hidden.astype(F32) > 0.0, grad_hidden, 0.0).astype(BF16)
            part1 = dot_nt(grad_pre, padded_rows(high, low))
            part2 = dot_nt(hidden, padded_rows(g_high, g_low))
            sum1 = part1 if sum1 is None else sum1 + part1
            sum2 = part2 if sum2 is None else sum2 + part2
        acc1_ref[...] += sum1
        acc2_ref[...] += sum2
        return carry

    lax.fori_loop(0, hidden_count, one_slice, 0)

    def folded(ref):
        return ref[:, 0:LANES] + ref[:, LANES : 2 * LANES]

    total = gather_taps(
        ((folded(acc1_ref), first_column, True), (folded(acc2_ref), second_column, False)), channels
    )
    lane = iota((channels, LANES), 1)
    diagonal = lane == iota((channels, LANES), 0)
    line = jnp.sum(jnp.where(diagonal, total[:, TAPS : TAPS + 1], 0.0), axis=0, keepdims=True)
    line = jnp.where(lane[0:8] == LOSS_AT, loss, jnp.broadcast_to(line, (8, LANES)))
    out_ref[0:channels, :] = total
    out_ref[channels : channels + 8, :] = jnp.where(lane[0:8] == GRAD_B_SECOND_AT, grad_b2, line)


def backward(shifted, hidden, pred, target, second, cells):
    height = second.shape[0]
    return pl.pallas_call(
        functools.partial(backward_kernel, cells),
        out_shape=(
            jax.ShapeDtypeStruct((height // Y + 8, LANES), F32),
            jax.ShapeDtypeStruct(target.shape, F32),
        ),
        in_specs=[VMEM] * 5,
        out_specs=(VMEM, VMEM),
        scratch_shapes=[
            pltpu.VMEM(shifted.shape, F32),
            pltpu.VMEM((height, 2 * LANES), F32),
            pltpu.VMEM((height, 2 * LANES), F32),
        ],
        compiler_params=vmem_mib(18),
        name="backward",
    )(shifted, hidden, pred, target, second)


def finish_kernel(one_ref, two_ref, loss_ref, w1_ref, b1_ref, w2_ref, b2_ref):
    total = one_ref[...] + two_ref[...]
    channels = w1_ref.shape[0]
    line = total[channels : channels + 1]
    loss_ref[...] = line[:, LOSS_AT : LOSS_AT + 1]
    w1_ref[...] = total[0:channels, 0:TAPS]
    b1_ref[...] = line[:, 0:channels]
    w2_ref[...] = total[0:channels, W_SECOND_AT : W_SECOND_AT + TAPS]
    b2_ref[...] = line[:, GRAD_B_SECOND_AT : GRAD_B_SECOND_AT + 1]


def sum_everywhere(value, channels):
    devices = lax.axis_size("subset") * lax.axis_size("slab")
    apart = 1
    while True:
        arrived = lax.ppermute(value, BOTH, [(i, i ^ apart) for i in range(devices)])
        apart *= 2
        if apart == devices:
            break
        value = value + arrived
    shapes = ((1, 1), (channels, TAPS), (1, channels), (channels, TAPS), (1, 1))
    return pl.pallas_call(
        finish_kernel,
        out_shape=tuple(jax.ShapeDtypeStruct(shape, F32) for shape in shapes),
        in_specs=[VMEM, VMEM],
        out_specs=(VMEM,) * 5,
        compiler_params=vmem_mib(1),
        name="finish",
    )(value, arrived)


def body(sinogram, angles, w_first, b_first, w_second, b_second):
    n_sub = lax.axis_size("subset") // 2
    n_slab = lax.axis_size("slab")
    devices = 2 * n_sub * n_slab
    group = 2 * n_slab
    local_views, z_count = sinogram.shape[0], sinogram.shape[1]
    depth = z_count // group
    channels = w_first.shape[0]
    scale = math.pi / (local_views * group)
    cells = float(n_sub * z_count * Y * X)
    assert devices & (devices - 1) == 0 and channels == 32 and depth >= HALO

    params = jnp.concatenate(
        [
            w_first,
            b_first[:, None],
            jnp.zeros((channels, W_SECOND_AT - TAPS - 1), F32),
            w_second,
            jnp.broadcast_to(b_second, (channels, LANES - W_SECOND_AT - TAPS)),
        ],
        axis=1,
    )
    first, second, turned = weights(params)
    sent = pack(angles, sinogram, group, depth)
    groups = [list(range(s * group, (s + 1) * group)) for s in range(n_sub)]
    got = lax.all_to_all(sent, BOTH, 0, 0, axis_index_groups=groups)
    got = got.reshape(group * local_views, depth + 2 * HALO, DW)
    ext, own = project(got, scale)

    others = None
    for apart in range(1, n_sub):
        pairs = [(i, (i + apart * group) % devices) for i in range(devices)]
        arrived = lax.ppermute(own, BOTH, pairs)
        others = arrived if others is None else others + arrived
    target = others if n_sub == 2 else others / (n_sub - 1)

    pred, again, shifted, hidden = forward(ext, params, first, turned)
    partial, target = backward(shifted, hidden, again, target, second, cells)
    loss, grad_w1, grad_b1, grad_w2, grad_b2 = sum_everywhere(partial, channels)
    return (
        pred[None],
        target[None],
        loss.reshape(()),
        grad_w1,
        grad_b1.reshape(-1),
        grad_w2,
        grad_b2.reshape(-1),
    )


def solution(mesh):
    return jax.shard_map(
        body,
        mesh=mesh,
        in_specs=(P(BOTH, None, None), P(BOTH), P(), P(), P(), P()),
        out_specs=(
            P("subset", "slab", None, None),
            P("subset", "slab", None, None),
            P(),
            P(),
            P(),
            P(),
            P(),
        ),
        check_vma=False,
    )
```

```python
import functools
import math

import jax
import jax.numpy as jnp
from jax import lax
from jax.experimental import pallas as pl
from jax.experimental.pallas import tpu as pltpu
from jax.sharding import PartitionSpec as P

DET = 2048
X = 1024
Y = 8
LANES = 128
TAPS = 27
TILE = 256
BLOCK = 80
W_SECOND_AT = 32
B_SECOND_AT = 59
LOSS_AT = 64
GRAD_B_SECOND_AT = 65
HALO = 2
BOTH = ("subset", "slab")

RADIUS = math.hypot((X - 1) / 2.0, (Y - 1) / 2.0) + 0.25
FIRST_D = math.floor((DET - 1) / 2.0 - RADIUS)
LAST_D = math.floor((DET - 1) / 2.0 + RADIUS) + 1
D0 = FIRST_D // LANES * LANES
DW = -(-(LAST_D + 1 - D0) // LANES) * LANES
assert FIRST_D - D0 >= 6 and D0 + DW <= DET

F32 = jnp.float32
BF16 = jnp.bfloat16
VMEM = pl.BlockSpec(memory_space=pltpu.VMEM)
SMEM = pl.BlockSpec(memory_space=pltpu.SMEM)


def vmem_mib(count):
    return pltpu.CompilerParams(vmem_limit_bytes=count * 2**20)


def iota(shape, dim):
    return lax.broadcasted_iota(jnp.int32, shape, dim)


def split2(value):
    high = value.astype(BF16)
    return high, (value - high.astype(F32)).astype(BF16)


def dot(a, b):
    return jnp.dot(a, b, preferred_element_type=F32)


def dot_nt(a, b):
    return lax.dot_general(a, b, (((1,), (1,)), ((), ())), preferred_element_type=F32)


def pack_kernel(depth, angle_ref, sino_ref, *refs):
    out_refs, (held_ref, rows_ref, cut_ref, sems) = refs[:-4], refs[-4:]
    views, z_count = sino_ref.shape[0], sino_ref.shape[1]
    n_slab = len(out_refs)
    rows = depth + 2 * HALO
    half = lax.axis_index("subset") % 2
    slab = lax.axis_index("slab")
    copies = [
        pltpu.make_async_copy(
            sino_ref.at[view, :, pl.ds(D0, DW)], held_ref.at[view], sems.at[view]
        )
        for view in range(views)
    ]
    for copy in copies:
        copy.start()
    lane = iota((rows, LANES), 1)
    zeros = jnp.zeros((8, DW), F32)
    rows_ref[0:8, :] = zeros
    rows_ref[8 + z_count : 16 + z_count, :] = zeros
    for view in range(views):
        angle = jnp.full((rows, LANES), angle_ref[view], F32)
        head = jnp.zeros((rows, LANES), F32)
        for which, left in enumerate((jnp.cos(angle), jnp.sin(angle))):
            for part in range(3):
                piece = left.astype(BF16).astype(F32)
                left = left - piece
                head = jnp.where(lane == 3 * which + part, piece, head)
        copies[view].wait()
        rows_ref[8 : 8 + z_count, :] = held_ref[view].astype(F32)
        for to in range(2 * n_slab):
            start = 8 + to * depth - HALO
            cut_ref[to] = rows_ref[start : start + rows, :]
            first = rows_ref[start : start + rows, 0:LANES]
            cut_ref[to, :, 0:LANES] = jnp.where(lane < 6, head, first)
        for apart, out_ref in enumerate(out_refs):
            to = jnp.bitwise_xor(slab, apart)
            mine = cut_ref[half * n_slab + to]
            other = cut_ref[(1 - half) * n_slab + to]
            out_ref[view] = jnp.concatenate([mine, other], axis=0).astype(BF16)


def pack(angles, sino, n_slab, depth):
    views, z_count = sino.shape[0], sino.shape[1]
    rows = depth + 2 * HALO
    return pl.pallas_call(
        functools.partial(pack_kernel, depth),
        out_shape=(jax.ShapeDtypeStruct((views, 2 * rows, DW), BF16),) * n_slab,
        in_specs=[SMEM, pl.BlockSpec(memory_space=pltpu.HBM)],
        out_specs=(VMEM,) * n_slab,
        scratch_shapes=[
            pltpu.VMEM((views, z_count, DW), BF16),
            pltpu.VMEM((z_count + 16, DW), F32),
            pltpu.VMEM((2 * n_slab, rows, DW), F32),
            pltpu.SemaphoreType.DMA((views,)),
        ],
        name="pack",
    )(angles, sino)


def project_kernel(count, scale, *refs):
    data_refs = refs[:count]
    init_refs = refs[count:-9]
    mine_ref, other_ref, own_ref, away_ref, low_ref, high_ref, tab_ref, scal_ref, sem = refs[-9:]
    each = data_refs[0].shape[0]
    views, rows = count * each, data_refs[0].shape[1]
    window = rows // 2
    centre = (DET - 1) / 2.0
    for place, data_ref in enumerate(data_refs):
        values = data_ref[...].astype(F32)
        moved = pltpu.roll(values.reshape(each * rows, DW), DW - 1, 1).reshape(values.shape)
        here = slice(place * each, (place + 1) * each)
        for tile in range(DW // LANES):
            cols = slice(tile * LANES, (tile + 1) * LANES)
            low_ref[here, tile] = values[:, :, cols]
            high_ref[here, tile] = moved[:, :, cols]
    head = low_ref[:, 0, 0, :]
    cosine = jnp.broadcast_to(head[:, 0:1] + head[:, 1:2] + head[:, 2:3], (views, LANES))
    sine = jnp.broadcast_to(head[:, 3:4] + head[:, 4:5] + head[:, 5:6], (views, LANES))

    def at(col, row):
        return col * cosine + row * sine + centre

    start = (iota((views, LANES), 1) % (X // LANES)).astype(F32) * LANES - (X - 1) / 2.0
    stop = start + (LANES - 1.0)
    edge = (Y - 1) / 2.0
    least = jnp.minimum(
        jnp.minimum(at(start, -edge), at(stop, -edge)), jnp.minimum(at(start, edge), at(stop, edge))
    )
    tab_ref[0] = cosine
    tab_ref[1] = sine
    tab_ref[2] = ((jnp.floor(least).astype(jnp.int32) - D0) // LANES).astype(F32)
    copy = pltpu.make_async_copy(tab_ref, scal_ref, sem)
    copy.start()
    copy.wait()

    lane = iota((views, LANES), 1)
    row_of_lane = (lane // (X // LANES) % Y).astype(F32) - edge
    ends = jnp.floor(at(stop, row_of_lane)) - jnp.floor(at(start, row_of_lane))
    apart = jnp.max(jnp.abs(ends)) >= float(LANES)

    lanes = iota((Y, LANES), 1)
    column = lanes.astype(F32)
    row_pos = iota((Y, LANES), 0).astype(F32) - edge

    def all_blocks(distinct):
        def one_block(block, carry):
            left = block.astype(F32) * LANES - (X - 1) / 2.0
            col = column + left

            def one_view(view, sums):
                tile = scal_ref[2, view, block].astype(jnp.int32)
                cos_part = scal_ref[0, view, 0]
                sin_part = row_pos * scal_ref[1, view, 0]
                position = col * cos_part + sin_part + centre
                lower = jnp.floor(position)
                weight_low = jnp.maximum(0.0, 1.0 - jnp.abs(position - lower))
                weight_high = jnp.maximum(0.0, 1.0 - jnp.abs(position - (lower + 1.0)))
                weight_low = weight_low.astype(BF16).astype(F32)
                weight_high = weight_high.astype(BF16).astype(F32)
                base = D0 + tile * LANES
                index = lower.astype(jnp.int32) - base
                second = index >= LANES
                index = jnp.bitwise_and(index, LANES - 1)
                if distinct:
                    end1 = left * cos_part + sin_part + centre
                    end2 = (left + (LANES - 1.0)) * cos_part + sin_part + centre
                    least_index = jnp.floor(jnp.minimum(end1, end2)).astype(jnp.int32) - base
                    in_first = lanes >= least_index

                def take(ref, z):
                    def line(at_tile):
                        return ref[view, at_tile, pl.ds(z, Y, stride=0), :]

                    def pick(values):
                        return jnp.take_along_axis(
                            values, index, axis=1, mode="promise_in_bounds"
                        )

                    one, two = line(tile), line(tile + 1)
                    if distinct:
                        return pick(jnp.where(in_first, one, two))
                    return jnp.where(second, pick(two), pick(one))

                return tuple(
                    sums[z] + (weight_low * take(low_ref, z) + weight_high * take(high_ref, z))
                    for z in range(rows)
                )

            cols = pl.ds(pl.multiple_of(block * LANES, LANES), LANES)
            if init_refs:
                sums = tuple(
                    init_refs[z // window][z % window, :, cols] for z in range(rows)
                )
            else:
                sums = tuple(jnp.zeros((Y, LANES), F32) for _ in range(rows))
            sums = lax.fori_loop(0, views, one_view, sums, unroll=views if distinct else 1)
            for z in range(rows):
                done = sums[z] * scale if scale else sums[z]
                at_z = z % window
                (mine_ref, other_ref)[z // window][at_z, :, cols] = done
                if scale and HALO <= at_z < window - HALO:
                    (own_ref, away_ref)[z // window][at_z - HALO, :, cols] = done
            return carry

        lax.fori_loop(0, X // LANES, one_block, 0)

    pl.when(apart)(lambda: all_blocks(False))
    pl.when(jnp.logical_not(apart))(lambda: all_blocks(True))


def project(chunks, init, scale):
    count = len(chunks)
    views, rows = count * chunks[0].shape[0], chunks[0].shape[1]
    whole = jax.ShapeDtypeStruct((rows // 2, Y, X), F32)
    inner = jax.ShapeDtypeStruct((rows // 2 - 2 * HALO if scale else 1, Y, X), F32)
    return pl.pallas_call(
        functools.partial(project_kernel, count, scale),
        out_shape=(whole, whole, inner, inner),
        in_specs=[VMEM] * (count + len(init)),
        out_specs=(VMEM,) * 4,
        scratch_shapes=[
            pltpu.VMEM((views, DW // LANES, rows, LANES), F32),
            pltpu.VMEM((views, DW // LANES, rows, LANES), F32),
            pltpu.VMEM((3, views, LANES), F32),
            pltpu.SMEM((3, views, LANES), F32),
            pltpu.SemaphoreType.DMA,
        ],
        compiler_params=vmem_mib(14),
        cost_estimate=pl.CostEstimate(
            flops=4_000_000_000, bytes_accessed=1_500_000, transcendentals=0
        ),
        name="project",
    )(*chunks, *init)


def select_taps(shape, rows_first, dy, column_of):
    param = iota(shape, 0 if rows_first else 1)
    row = iota(shape, 1 if rows_first else 0)
    row = row % BLOCK
    return param, row, column_of(row // 24, (row // 8) % 3, dy)


def first_column(dx, dz, dy):
    return 9 * dz + 3 * dy + dx


def second_column(dx, dz, dy):
    return W_SECOND_AT + (TAPS - 1) - first_column(dx, dz, dy)


def spread(params, column_of, bias):
    channels = params.shape[0]
    height = channels * Y
    high, low = split2(params)
    both = jnp.concatenate([high, low], axis=1)
    rep = (iota((height, channels), 0) // Y == iota((height, channels), 1)).astype(F32)
    rep = rep.astype(BF16)
    shape = (2 * LANES, TILE)
    source = iota(shape, 0)
    col = iota(shape, 1)
    part, inner = col // BLOCK, col % BLOCK
    wanted_half = jnp.where(part == 2, 1, 0)
    usable = (part < 3) & (source // LANES == wanted_half)
    out_col = iota((height, TILE), 1)
    out_inner = out_col % BLOCK
    out_y = iota((height, TILE), 0) % Y
    total = jnp.zeros((height, TILE), F32)
    for dy in range(3):
        wanted = column_of(inner // 24, (inner // 8) % 3, dy)
        pick = usable & (inner < 72) & (source % LANES == wanted)
        if bias and dy == 1:
            pick = pick | (usable & (inner == 72) & (source % LANES == TAPS))
        chosen = dot(both, pick.astype(F32).astype(BF16)).astype(BF16)
        here = (out_inner < 72) & (out_inner % 8 - out_y + 1 == dy)
        if bias and dy == 1:
            here = here | (out_inner == 72)
        total = total + jnp.where(here, dot(rep, chosen), 0.0)
    return total.astype(BF16)


def gather_taps(grads, channels):
    height = channels * Y
    col = iota((height, LANES), 1)
    row_y = iota((height, LANES), 0) % Y
    inner = iota((LANES, LANES), 0)
    to = iota((LANES, LANES), 1)
    pieces = []
    picks = []
    for grad, column_of, bias in grads:
        for dy in range(3):
            here = (col < 72) & (col % 8 - row_y + 1 == dy)
            pick = (inner < 72) & (to == column_of(inner // 24, (inner // 8) % 3, dy))
            if bias and dy == 1:
                here = here | (col == 72)
                pick = pick | ((inner == 72) & (to == TAPS))
            masked = jnp.where(here, grad, 0.0).reshape(channels, Y, LANES)
            pieces.append(jnp.sum(masked, axis=1))
            picks.append(pick.astype(F32))
    return jnp.dot(
        jnp.concatenate(pieces, axis=1),
        jnp.concatenate(picks, axis=0),
        precision=lax.Precision.HIGHEST,
        preferred_element_type=F32,
    )


def shift_columns(value, by):
    if by == 0:
        return value
    rolled = pltpu.roll(value, (-by) % X, 1)
    lane = iota(value.shape, 1)
    return jnp.where(lane == (X - 1 if by > 0 else 0), 0.0, rolled)


def fill_shifted(ref, field):
    for dx in range(3):
        ref[dx] = shift_columns(field, dx - 1)


def patch(ref, slice_index, tile):
    at = pl.multiple_of(slice_index * Y, Y)
    cols = slice(tile * TILE, (tile + 1) * TILE)
    pieces = [ref[dx, pl.ds(at, 3 * Y), cols] for dx in range(3)]
    pieces.append((iota((8, TILE), 0) == 0).astype(F32))
    high, low = split2(jnp.concatenate(pieces, axis=0))
    return high, low


def apply_spread(weights, high, low):
    return dot(weights[:, 0 : 3 * BLOCK], jnp.concatenate([high, low, high], axis=0))


def slice_flag(hidden_slice, hidden_count):
    n_slab = lax.axis_size("slab")
    place = (lax.axis_index("subset") % 2) * n_slab + lax.axis_index("slab")
    outside = ((hidden_slice == 0) & (place == 0)) | (
        (hidden_slice == hidden_count - 1) & (place == 2 * n_slab - 1)
    )
    return jnp.where(outside, 0.0, 1.0).astype(F32)


def weights_kernel(params_ref, first_ref, second_ref, turned_ref):
    params = params_ref[...]
    second = spread(params, second_column, False)
    first_ref[...] = spread(params, first_column, True)
    second_ref[...] = second
    turned_ref[...] = second.astype(F32).T.astype(BF16)


def weights(params):
    height = params.shape[0] * Y
    return pl.pallas_call(
        weights_kernel,
        out_shape=(
            jax.ShapeDtypeStruct((height, TILE), BF16),
            jax.ShapeDtypeStruct((height, TILE), BF16),
            jax.ShapeDtypeStruct((TILE, height), BF16),
        ),
        in_specs=[VMEM],
        out_specs=(VMEM,) * 3,
        compiler_params=vmem_mib(8),
        name="weights",
    )(params)


def forward_kernel(
    mine_ref,
    came_ref,
    params_ref,
    first_ref,
    turned_ref,
    pred_ref,
    again_ref,
    shifted_ref,
    hidden_ref,
    acc_ref,
):
    rows = mine_ref.shape[0]
    hidden_count = rows - 2
    height = first_ref.shape[0]
    first = first_ref[...]
    fill_shifted(shifted_ref, (mine_ref[...] + came_ref[...]).reshape(rows * Y, X))
    acc_ref[...] = jnp.zeros(acc_ref.shape, F32)

    def one_slice(hidden_slice, carry):
        flag = slice_flag(hidden_slice, hidden_count)
        at = pl.multiple_of(hidden_slice * Y, Y)
        kept = pl.ds(pl.multiple_of(hidden_slice * height, height), height)
        for tile in range(X // TILE):
            cols = slice(tile * TILE, (tile + 1) * TILE)
            high, low = patch(shifted_ref, hidden_slice, tile)
            hidden = jnp.maximum(apply_spread(first, high, low), 0.0) * flag
            h_high, h_low = split2(hidden)
            hidden_ref[kept, cols] = h_high
            main = dot(turned_ref[BLOCK : 3 * BLOCK], h_high)
            taps = main[0:BLOCK] + main[BLOCK : 2 * BLOCK] + dot(turned_ref[0:BLOCK], h_low)
            for dx in range(3):
                acc_ref[dx, pl.ds(at, 3 * Y), cols] += taps[24 * dx : 24 * dx + 24]
        return carry

    lax.fori_loop(0, hidden_count, one_slice, 0)
    inner = slice(HALO * Y, (rows - HALO) * Y)
    added = acc_ref[1, inner, :]
    for dx in (0, 2):
        added = added + shift_columns(acc_ref[dx, inner, :], 1 - dx)
    own = shifted_ref[1, inner, :]
    bias = params_ref[0:1, B_SECOND_AT : B_SECOND_AT + 1]
    pred = (own + added + bias).reshape(pred_ref.shape)
    pred_ref[...] = pred
    again_ref[...] = pred


def forward(mine, came, params, first, turned):
    rows = mine.shape[0]
    height = first.shape[0]
    own = jax.ShapeDtypeStruct((rows - 2 * HALO, Y, X), F32)
    return pl.pallas_call(
        forward_kernel,
        out_shape=(
            own,
            own,
            jax.ShapeDtypeStruct((3, rows * Y, X), F32),
            jax.ShapeDtypeStruct(((rows - 2) * height, X), BF16),
        ),
        in_specs=[VMEM] * 5,
        out_specs=(VMEM,) * 4,
        scratch_shapes=[pltpu.VMEM((3, rows * Y, X), F32)],
        cost_estimate=pl.CostEstimate(
            flops=20_000_000_000, bytes_accessed=2_000_000, transcendentals=0
        ),
        compiler_params=vmem_mib(18),
        name="forward",
    )(mine, came, params, first, turned)


def padded_rows(high, low):
    none = jnp.zeros((LANES - BLOCK, high.shape[1]), BF16)
    return jnp.concatenate([high, none, low, none], axis=0)


def backward_kernel(cells, others, shifted_ref, hidden_ref, pred_ref, second_ref, *refs):
    part_refs = refs[: 2 * others]
    out_ref, target_out_ref, grad_ref, acc1_ref, acc2_ref = refs[2 * others :]
    rows = shifted_ref.shape[1] // Y
    hidden_count = rows - 2
    height = second_ref.shape[0]
    channels = height // Y
    target = part_refs[0][...]
    for part_ref in part_refs[1:]:
        target = target + part_ref[...]
    target = target if others == 1 else target / others
    target_out_ref[...] = target
    diff = (pred_ref[...] - target).reshape((rows - 2 * HALO) * Y, X)
    resid = 2.0 * diff / cells
    loss = jnp.sum(diff * diff, keepdims=True) / cells
    grad_b2 = jnp.sum(resid, keepdims=True)
    inner = slice(HALO * Y, (rows - HALO) * Y)
    for dx in range(3):
        grad_ref[dx, 0 : HALO * Y, :] = jnp.zeros((HALO * Y, X), F32)
        grad_ref[dx, (rows - HALO) * Y : rows * Y, :] = jnp.zeros((HALO * Y, X), F32)
        grad_ref[dx, inner, :] = shift_columns(resid, dx - 1)
    acc1_ref[...] = jnp.zeros(acc1_ref.shape, F32)
    acc2_ref[...] = jnp.zeros(acc2_ref.shape, F32)
    second = second_ref[...]

    def one_slice(hidden_slice, carry):
        kept = pl.ds(pl.multiple_of(hidden_slice * height, height), height)
        sum1 = None
        sum2 = None
        for tile in range(X // TILE):
            cols = slice(tile * TILE, (tile + 1) * TILE)
            high, low = patch(shifted_ref, hidden_slice, tile)
            g_high, g_low = patch(grad_ref, hidden_slice, tile)
            hidden = hidden_ref[kept, cols]
            grad_hidden = apply_spread(second, g_high, g_low)
            grad_pre = jnp.where(hidden.astype(F32) > 0.0, grad_hidden, 0.0).astype(BF16)
            part1 = dot_nt(grad_pre, padded_rows(high, low))
            part2 = dot_nt(hidden, padded_rows(g_high, g_low))
            sum1 = part1 if sum1 is None else sum1 + part1
            sum2 = part2 if sum2 is None else sum2 + part2
        acc1_ref[...] += sum1
        acc2_ref[...] += sum2
        return carry

    lax.fori_loop(0, hidden_count, one_slice, 0)

    def folded(ref):
        return ref[:, 0:LANES] + ref[:, LANES : 2 * LANES]

    total = gather_taps(
        ((folded(acc1_ref), first_column, True), (folded(acc2_ref), second_column, False)), channels
    )
    lane = iota((channels, LANES), 1)
    diagonal = lane == iota((channels, LANES), 0)
    line = jnp.sum(jnp.where(diagonal, total[:, TAPS : TAPS + 1], 0.0), axis=0, keepdims=True)
    line = jnp.where(lane[0:8] == LOSS_AT, loss, jnp.broadcast_to(line, (8, LANES)))
    out_ref[0:channels, :] = total
    out_ref[channels : channels + 8, :] = jnp.where(lane[0:8] == GRAD_B_SECOND_AT, grad_b2, line)


def backward(shifted, hidden, pred, parts, second, cells):
    height = second.shape[0]
    return pl.pallas_call(
        functools.partial(backward_kernel, cells, len(parts) // 2),
        out_shape=(
            jax.ShapeDtypeStruct((height // Y + 8, LANES), F32),
            jax.ShapeDtypeStruct(pred.shape, F32),
        ),
        in_specs=[VMEM] * (4 + len(parts)),
        out_specs=(VMEM, VMEM),
        scratch_shapes=[
            pltpu.VMEM(shifted.shape, F32),
            pltpu.VMEM((height, 2 * LANES), F32),
            pltpu.VMEM((height, 2 * LANES), F32),
        ],
        compiler_params=vmem_mib(18),
        name="backward",
    )(shifted, hidden, pred, second, *parts)


def finish_kernel(one_ref, two_ref, loss_ref, w1_ref, b1_ref, w2_ref, b2_ref):
    total = one_ref[...] + two_ref[...]
    channels = w1_ref.shape[0]
    line = total[channels : channels + 1]
    loss_ref[...] = line[:, LOSS_AT : LOSS_AT + 1]
    w1_ref[...] = total[0:channels, 0:TAPS]
    b1_ref[...] = line[:, 0:channels]
    w2_ref[...] = total[0:channels, W_SECOND_AT : W_SECOND_AT + TAPS]
    b2_ref[...] = line[:, GRAD_B_SECOND_AT : GRAD_B_SECOND_AT + 1]


def sum_everywhere(value, channels):
    devices = lax.axis_size("subset") * lax.axis_size("slab")
    apart = 1
    while True:
        arrived = lax.ppermute(value, BOTH, [(i, i ^ apart) for i in range(devices)])
        apart *= 2
        if apart == devices:
            break
        value = value + arrived
    shapes = ((1, 1), (channels, TAPS), (1, channels), (channels, TAPS), (1, 1))
    return pl.pallas_call(
        finish_kernel,
        out_shape=tuple(jax.ShapeDtypeStruct(shape, F32) for shape in shapes),
        in_specs=[VMEM, VMEM],
        out_specs=(VMEM,) * 5,
        compiler_params=vmem_mib(1),
        name="finish",
    )(value, arrived)


def send_order(n_slab):
    return list(range(n_slab // 2, n_slab)) + list(range(1, n_slab // 2))


def body(sinogram, angles, w_first, b_first, w_second, b_second):
    n_sub = lax.axis_size("subset") // 2
    n_slab = lax.axis_size("slab")
    devices = 2 * n_sub * n_slab
    group = 2 * n_slab
    local_views, z_count = sinogram.shape[0], sinogram.shape[1]
    depth = z_count // group
    channels = w_first.shape[0]
    scale = math.pi / (local_views * group)
    cells = float(n_sub * z_count * Y * X)
    assert devices & (devices - 1) == 0 and n_slab > 1 and channels == 32 and depth >= HALO

    params = jnp.concatenate(
        [
            w_first,
            b_first[:, None],
            jnp.zeros((channels, W_SECOND_AT - TAPS - 1), F32),
            w_second,
            jnp.broadcast_to(b_second, (channels, LANES - W_SECOND_AT - TAPS)),
        ],
        axis=1,
    )
    first, second, turned = weights(params)
    sent = pack(angles, sinogram, n_slab, depth)

    def exchange(value, distance):
        return lax.ppermute(value, BOTH, [(i, i ^ distance) for i in range(devices)])

    arrived = [sent[0]] + [None] * (n_slab - 1)
    for distance in send_order(n_slab):
        arrived[distance] = exchange(sent[distance], distance)
    near = n_slab // 2
    sums = project(arrived[:near], (), 0.0)
    mine, other, own, away = project(arrived[near:], sums[:2], scale)
    came = exchange(other, n_slab)
    parts = []
    for apart in range(1, n_sub):
        straight = [(i, (i + apart * group) % devices) for i in range(devices)]
        crossed = [(i, j ^ n_slab) for i, j in straight]
        parts.append(lax.ppermute(own, BOTH, straight))
        parts.append(lax.ppermute(away, BOTH, crossed))

    pred, again, shifted, hidden = forward(mine, came, params, first, turned)
    partial, target = backward(shifted, hidden, again, parts, second, cells)
    loss, grad_w1, grad_b1, grad_w2, grad_b2 = sum_everywhere(partial, channels)
    return (
        pred[None],
        target[None],
        loss.reshape(()),
        grad_w1,
        grad_b1.reshape(-1),
        grad_w2,
        grad_b2.reshape(-1),
    )


def solution(mesh):
    return jax.shard_map(
        body,
        mesh=mesh,
        in_specs=(P(BOTH, None, None), P(BOTH), P(), P(), P(), P()),
        out_specs=(
            P("subset", "slab", None, None),
            P("subset", "slab", None, None),
            P(),
            P(),
            P(),
            P(),
            P(),
        ),
        check_vma=False,
    )
```

```python
import functools
import math

import jax
import jax.numpy as jnp
from jax import lax
from jax.experimental import pallas as pl
from jax.experimental.pallas import tpu as pltpu
from jax.sharding import PartitionSpec as P


DET = 2048
X = 1024
Y = 8
LANES = 128
TAPS = 27
TILE = 256
BLOCK = 80
W_SECOND_AT = 32
B_SECOND_AT = 59
LOSS_AT = 64
GRAD_B_SECOND_AT = 65
HALO = 2
BOTH = ("subset", "slab")

RADIUS = math.hypot((X - 1) / 2.0, (Y - 1) / 2.0) + 0.25
FIRST_D = math.floor((DET - 1) / 2.0 - RADIUS)
LAST_D = math.floor((DET - 1) / 2.0 + RADIUS) + 1
D0 = FIRST_D - 8
DW = -(-(LAST_D + 1 - D0) // LANES) * LANES
READ_D = D0 // LANES * LANES
READ_W = -(-(D0 + DW - READ_D) // LANES) * LANES
assert D0 >= 0 and READ_D + READ_W <= DET

F32 = jnp.float32
BF16 = jnp.bfloat16
VMEM = pl.BlockSpec(memory_space=pltpu.VMEM)
SMEM = pl.BlockSpec(memory_space=pltpu.SMEM)


def vmem_mib(count):
    return pltpu.CompilerParams(vmem_limit_bytes=count * 2**20)


def iota(shape, dim):
    return lax.broadcasted_iota(jnp.int32, shape, dim)


def split2(value):
    high = value.astype(BF16)
    return high, (value - high.astype(F32)).astype(BF16)


def dot(a, b):
    return jnp.dot(a, b, preferred_element_type=F32)


def dot_nt(a, b):
    return lax.dot_general(a, b, (((1,), (1,)), ((), ())), preferred_element_type=F32)


def pack_kernel(depth, angle_ref, sino_ref, *refs):
    out_refs, (held_ref, rows_ref, cut_ref, sems) = refs[:-4], refs[-4:]
    views, z_count = sino_ref.shape[0], sino_ref.shape[1]
    n_slab = len(out_refs)
    rows = depth + 2 * HALO
    half = lax.axis_index("subset") % 2
    slab = lax.axis_index("slab")
    copies = [
        pltpu.make_async_copy(
            sino_ref.at[view, :, pl.ds(READ_D, READ_W)], held_ref.at[view], sems.at[view]
        )
        for view in range(views)
    ]
    for copy in copies:
        copy.start()
    lane = iota((rows, LANES), 1)
    zeros = jnp.zeros((8, DW), F32)
    rows_ref[0:8, :] = zeros
    rows_ref[8 + z_count : 16 + z_count, :] = zeros
    for view in range(views):
        angle = jnp.full((rows, LANES), angle_ref[view], F32)
        head = jnp.zeros((rows, LANES), F32)
        for which, left in enumerate((jnp.cos(angle), jnp.sin(angle))):
            for part in range(3):
                piece = left.astype(BF16).astype(F32)
                left = left - piece
                head = jnp.where(lane == 3 * which + part, piece, head)
        copies[view].wait()
        moved = pltpu.roll(held_ref[view].astype(F32), (READ_D - D0) % READ_W, 1)
        rows_ref[8 : 8 + z_count, :] = moved[:, 0:DW]
        for to in range(2 * n_slab):
            start = 8 + to * depth - HALO
            cut_ref[to] = rows_ref[start : start + rows, :]
            first = rows_ref[start : start + rows, 0:LANES]
            cut_ref[to, :, 0:LANES] = jnp.where(lane < 6, head, first)
        for apart, out_ref in enumerate(out_refs):
            to = jnp.bitwise_xor(slab, apart)
            mine = cut_ref[half * n_slab + to]
            other = cut_ref[(1 - half) * n_slab + to]
            out_ref[view] = jnp.concatenate([mine, other], axis=0).astype(BF16)


def pack(angles, sino, n_slab, depth):
    views, z_count = sino.shape[0], sino.shape[1]
    rows = depth + 2 * HALO
    return pl.pallas_call(
        functools.partial(pack_kernel, depth),
        out_shape=(jax.ShapeDtypeStruct((views, 2 * rows, DW), BF16),) * n_slab,
        in_specs=[SMEM, pl.BlockSpec(memory_space=pltpu.HBM)],
        out_specs=(VMEM,) * n_slab,
        scratch_shapes=[
            pltpu.VMEM((views, z_count, READ_W), BF16),
            pltpu.VMEM((z_count + 16, DW), F32),
            pltpu.VMEM((2 * n_slab, rows, DW), F32),
            pltpu.SemaphoreType.DMA((views,)),
        ],
        compiler_params=vmem_mib(8),
        name="pack",
    )(
        pltpu.with_memory_space_constraint(angles, pltpu.HBM),
        pltpu.with_memory_space_constraint(sino, pltpu.HBM),
    )


def project_kernel(count, scale, *refs):
    data_refs = refs[:count]
    init_refs = refs[count:-9]
    mine_ref, other_ref, own_ref, away_ref, low_ref, high_ref, tab_ref, scal_ref, sem = refs[-9:]
    each = data_refs[0].shape[0]
    views, rows = count * each, data_refs[0].shape[1]
    window = rows // 2
    centre = (DET - 1) / 2.0
    for place, data_ref in enumerate(data_refs):
        values = data_ref[...].astype(F32)
        moved = pltpu.roll(values.reshape(each * rows, DW), DW - 1, 1).reshape(values.shape)
        here = slice(place * each, (place + 1) * each)
        for tile in range(DW // LANES):
            cols = slice(tile * LANES, (tile + 1) * LANES)
            low_ref[here, tile] = values[:, :, cols]
            high_ref[here, tile] = moved[:, :, cols]
    head = low_ref[:, 0, 0, :]
    cosine = jnp.broadcast_to(head[:, 0:1] + head[:, 1:2] + head[:, 2:3], (views, LANES))
    sine = jnp.broadcast_to(head[:, 3:4] + head[:, 4:5] + head[:, 5:6], (views, LANES))

    def at(col, row):
        return col * cosine + row * sine + centre

    start = (iota((views, LANES), 1) % (X // LANES)).astype(F32) * LANES - (X - 1) / 2.0
    stop = start + (LANES - 1.0)
    edge = (Y - 1) / 2.0
    least = jnp.minimum(
        jnp.minimum(at(start, -edge), at(stop, -edge)), jnp.minimum(at(start, edge), at(stop, edge))
    )
    tab_ref[0] = cosine
    tab_ref[1] = sine
    tab_ref[2] = ((jnp.floor(least).astype(jnp.int32) - D0) // LANES).astype(F32)
    copy = pltpu.make_async_copy(tab_ref, scal_ref, sem)
    copy.start()
    copy.wait()

    lane = iota((views, LANES), 1)
    row_of_lane = (lane // (X // LANES) % Y).astype(F32) - edge
    ends = jnp.floor(at(stop, row_of_lane)) - jnp.floor(at(start, row_of_lane))
    apart = jnp.max(jnp.abs(ends)) >= float(LANES)

    lanes = iota((Y, LANES), 1)
    column = lanes.astype(F32)
    row_pos = iota((Y, LANES), 0).astype(F32) - edge

    def all_blocks(distinct):
        def one_block(block, carry):
            left = block.astype(F32) * LANES - (X - 1) / 2.0
            col = column + left

            def one_view(view, sums):
                tile = scal_ref[2, view, block].astype(jnp.int32)
                cos_part = scal_ref[0, view, 0]
                sin_part = row_pos * scal_ref[1, view, 0]
                position = col * cos_part + sin_part + centre
                lower = jnp.floor(position)
                weight_low = jnp.maximum(0.0, 1.0 - jnp.abs(position - lower))
                weight_high = jnp.maximum(0.0, 1.0 - jnp.abs(position - (lower + 1.0)))
                weight_low = weight_low.astype(BF16).astype(F32)
                weight_high = weight_high.astype(BF16).astype(F32)
                base = D0 + tile * LANES
                index = lower.astype(jnp.int32) - base
                second = index >= LANES
                index = jnp.bitwise_and(index, LANES - 1)
                if distinct:
                    end1 = left * cos_part + sin_part + centre
                    end2 = (left + (LANES - 1.0)) * cos_part + sin_part + centre
                    least_index = jnp.floor(jnp.minimum(end1, end2)).astype(jnp.int32) - base
                    in_first = lanes >= least_index

                def take(ref, z):
                    def line(at_tile):
                        return ref[view, at_tile, pl.ds(z, Y, stride=0), :]

                    def pick(values):
                        return jnp.take_along_axis(
                            values, index, axis=1, mode="promise_in_bounds"
                        )

                    one, two = line(tile), line(tile + 1)
                    if distinct:
                        return pick(jnp.where(in_first, one, two))
                    return jnp.where(second, pick(two), pick(one))

                return tuple(
                    sums[z] + (weight_low * take(low_ref, z) + weight_high * take(high_ref, z))
                    for z in range(rows)
                )

            cols = pl.ds(pl.multiple_of(block * LANES, LANES), LANES)
            if init_refs:
                sums = tuple(
                    init_refs[z // window][z % window, :, cols] for z in range(rows)
                )
            else:
                sums = tuple(jnp.zeros((Y, LANES), F32) for _ in range(rows))
            sums = lax.fori_loop(0, views, one_view, sums, unroll=views if distinct else 1)
            for z in range(rows):
                done = sums[z] * scale if scale else sums[z]
                at_z = z % window
                (mine_ref, other_ref)[z // window][at_z, :, cols] = done
                if scale and HALO <= at_z < window - HALO:
                    (own_ref, away_ref)[z // window][at_z - HALO, :, cols] = done
            return carry

        lax.fori_loop(0, X // LANES, one_block, 0)

    pl.when(apart)(lambda: all_blocks(False))
    pl.when(jnp.logical_not(apart))(lambda: all_blocks(True))


def project(chunks, init, scale):
    count = len(chunks)
    views, rows = count * chunks[0].shape[0], chunks[0].shape[1]
    whole = jax.ShapeDtypeStruct((rows // 2, Y, X), F32)
    inner = jax.ShapeDtypeStruct((rows // 2 - 2 * HALO if scale else 1, Y, X), F32)
    return pl.pallas_call(
        functools.partial(project_kernel, count, scale),
        out_shape=(whole, whole, inner, inner),
        in_specs=[VMEM] * (count + len(init)),
        out_specs=(VMEM,) * 4,
        scratch_shapes=[
            pltpu.VMEM((views, DW // LANES, rows, LANES), F32),
            pltpu.VMEM((views, DW // LANES, rows, LANES), F32),
            pltpu.VMEM((3, views, LANES), F32),
            pltpu.SMEM((3, views, LANES), F32),
            pltpu.SemaphoreType.DMA,
        ],
        compiler_params=vmem_mib(14),
        cost_estimate=pl.CostEstimate(
            flops=4_000_000_000, bytes_accessed=1_500_000, transcendentals=0
        ),
        name="project",
    )(*chunks, *init)


def first_column(dx, dz, dy):
    return 9 * dz + 3 * dy + dx


def second_column(dx, dz, dy):
    return W_SECOND_AT + (TAPS - 1) - first_column(dx, dz, dy)


def spread(params, column_of, bias):
    channels = params.shape[0]
    height = channels * Y
    high, low = split2(params)
    both = jnp.concatenate([high, low], axis=1)
    rep = (iota((height, channels), 0) // Y == iota((height, channels), 1)).astype(F32)
    rep = rep.astype(BF16)
    shape = (2 * LANES, TILE)
    source = iota(shape, 0)
    col = iota(shape, 1)
    part, inner = col // BLOCK, col % BLOCK
    wanted_half = jnp.where(part == 2, 1, 0)
    usable = (part < 3) & (source // LANES == wanted_half)
    out_col = iota((height, TILE), 1)
    out_inner = out_col % BLOCK
    out_y = iota((height, TILE), 0) % Y
    total = jnp.zeros((height, TILE), F32)
    for dy in range(3):
        wanted = column_of(inner // 24, (inner // 8) % 3, dy)
        pick = usable & (inner < 72) & (source % LANES == wanted)
        if bias and dy == 1:
            pick = pick | (usable & (inner == 72) & (source % LANES == TAPS))
        chosen = dot(both, pick.astype(F32).astype(BF16)).astype(BF16)
        here = (out_inner < 72) & (out_inner % 8 - out_y + 1 == dy)
        if bias and dy == 1:
            here = here | (out_inner == 72)
        total = total + jnp.where(here, dot(rep, chosen), 0.0)
    return total.astype(BF16)


def gather_taps(grads, channels):
    height = channels * Y
    col = iota((height, LANES), 1)
    row_y = iota((height, LANES), 0) % Y
    inner = iota((LANES, LANES), 0)
    to = iota((LANES, LANES), 1)
    pieces = []
    picks = []
    for grad, column_of, bias in grads:
        for dy in range(3):
            here = (col < 72) & (col % 8 - row_y + 1 == dy)
            pick = (inner < 72) & (to == column_of(inner // 24, (inner // 8) % 3, dy))
            if bias and dy == 1:
                here = here | (col == 72)
                pick = pick | ((inner == 72) & (to == TAPS))
            masked = jnp.where(here, grad, 0.0).reshape(channels, Y, LANES)
            pieces.append(jnp.sum(masked, axis=1))
            picks.append(pick.astype(F32))
    return jnp.dot(
        jnp.concatenate(pieces, axis=1),
        jnp.concatenate(picks, axis=0),
        precision=lax.Precision.HIGHEST,
        preferred_element_type=F32,
    )


def shift_columns(value, by):
    if by == 0:
        return value
    rolled = pltpu.roll(value, (-by) % X, 1)
    lane = iota(value.shape, 1)
    return jnp.where(lane == (X - 1 if by > 0 else 0), 0.0, rolled)


def fill_shifted(ref, field):
    for dx in range(3):
        ref[dx] = shift_columns(field, dx - 1)


def patch(ref, slice_index, tile):
    at = pl.multiple_of(slice_index * Y, Y)
    cols = slice(tile * TILE, (tile + 1) * TILE)
    pieces = [ref[dx, pl.ds(at, 3 * Y), cols] for dx in range(3)]
    pieces.append((iota((8, TILE), 0) == 0).astype(F32))
    high, low = split2(jnp.concatenate(pieces, axis=0))
    return high, low


def apply_spread(weights, high, low):
    return dot(weights[:, 0 : 3 * BLOCK], jnp.concatenate([high, low, high], axis=0))


def slice_flag(hidden_slice, hidden_count):
    n_slab = lax.axis_size("slab")
    place = (lax.axis_index("subset") % 2) * n_slab + lax.axis_index("slab")
    outside = ((hidden_slice == 0) & (place == 0)) | (
        (hidden_slice == hidden_count - 1) & (place == 2 * n_slab - 1)
    )
    return jnp.where(outside, 0.0, 1.0).astype(F32)


def weights_kernel(params_ref, first_ref, second_ref, turned_ref):
    params = params_ref[...]
    second = spread(params, second_column, False)
    first_ref[...] = spread(params, first_column, True)
    second_ref[...] = second
    turned_ref[...] = second.astype(F32).T.astype(BF16)


def weights(params):
    height = params.shape[0] * Y
    return pl.pallas_call(
        weights_kernel,
        out_shape=(
            jax.ShapeDtypeStruct((height, TILE), BF16),
            jax.ShapeDtypeStruct((height, TILE), BF16),
            jax.ShapeDtypeStruct((TILE, height), BF16),
        ),
        in_specs=[VMEM],
        out_specs=(VMEM,) * 3,
        compiler_params=vmem_mib(8),
        name="weights",
    )(params)


def forward_kernel(
    mine_ref,
    came_ref,
    params_ref,
    first_ref,
    turned_ref,
    pred_ref,
    again_ref,
    shifted_ref,
    hidden_ref,
    acc_ref,
):
    rows = mine_ref.shape[0]
    hidden_count = rows - 2
    height = first_ref.shape[0]
    first = first_ref[...]
    fill_shifted(shifted_ref, (mine_ref[...] + came_ref[...]).reshape(rows * Y, X))
    acc_ref[...] = jnp.zeros(acc_ref.shape, F32)

    def one_slice(hidden_slice, carry):
        flag = slice_flag(hidden_slice, hidden_count)
        at = pl.multiple_of(hidden_slice * Y, Y)
        kept = pl.ds(pl.multiple_of(hidden_slice * height, height), height)
        for tile in range(X // TILE):
            cols = slice(tile * TILE, (tile + 1) * TILE)
            high, low = patch(shifted_ref, hidden_slice, tile)
            hidden = jnp.maximum(apply_spread(first, high, low), 0.0) * flag
            h_high, h_low = split2(hidden)
            hidden_ref[kept, cols] = h_high
            main = dot(turned_ref[BLOCK : 3 * BLOCK], h_high)
            taps = main[0:BLOCK] + main[BLOCK : 2 * BLOCK] + dot(turned_ref[0:BLOCK], h_low)
            for dx in range(3):
                acc_ref[dx, pl.ds(at, 3 * Y), cols] += taps[24 * dx : 24 * dx + 24]
        return carry

    lax.fori_loop(0, hidden_count, one_slice, 0)
    inner = slice(HALO * Y, (rows - HALO) * Y)
    added = acc_ref[1, inner, :]
    for dx in (0, 2):
        added = added + shift_columns(acc_ref[dx, inner, :], 1 - dx)
    own = shifted_ref[1, inner, :]
    bias = params_ref[0:1, B_SECOND_AT : B_SECOND_AT + 1]
    pred = (own + added + bias).reshape(pred_ref.shape)
    pred_ref[...] = pred
    again_ref[...] = pred


def forward(mine, came, params, first, turned):
    rows = mine.shape[0]
    height = first.shape[0]
    own = jax.ShapeDtypeStruct((rows - 2 * HALO, Y, X), F32)
    return pl.pallas_call(
        forward_kernel,
        out_shape=(
            own,
            own,
            jax.ShapeDtypeStruct((3, rows * Y, X), F32),
            jax.ShapeDtypeStruct(((rows - 2) * height, X), BF16),
        ),
        in_specs=[VMEM] * 5,
        out_specs=(VMEM,) * 4,
        scratch_shapes=[pltpu.VMEM((3, rows * Y, X), F32)],
        cost_estimate=pl.CostEstimate(
            flops=20_000_000_000, bytes_accessed=2_000_000, transcendentals=0
        ),
        compiler_params=vmem_mib(18),
        name="forward",
    )(mine, came, params, first, turned)


def padded_rows(high, low):
    none = jnp.zeros((LANES - BLOCK, high.shape[1]), BF16)
    return jnp.concatenate([high, none, low, none], axis=0)


def backward_kernel(cells, others, shifted_ref, hidden_ref, pred_ref, second_ref, *refs):
    part_refs = refs[: 2 * others]
    out_ref, target_out_ref, grad_ref, acc1_ref, acc2_ref = refs[2 * others :]
    rows = shifted_ref.shape[1] // Y
    hidden_count = rows - 2
    height = second_ref.shape[0]
    channels = height // Y
    target = part_refs[0][...]
    for part_ref in part_refs[1:]:
        target = target + part_ref[...]
    target = target if others == 1 else target / others
    target_out_ref[...] = target
    diff = (pred_ref[...] - target).reshape((rows - 2 * HALO) * Y, X)
    resid = 2.0 * diff / cells
    loss = jnp.sum(diff * diff, keepdims=True) / cells
    grad_b2 = jnp.sum(resid, keepdims=True)
    inner = slice(HALO * Y, (rows - HALO) * Y)
    for dx in range(3):
        grad_ref[dx, 0 : HALO * Y, :] = jnp.zeros((HALO * Y, X), F32)
        grad_ref[dx, (rows - HALO) * Y : rows * Y, :] = jnp.zeros((HALO * Y, X), F32)
        grad_ref[dx, inner, :] = shift_columns(resid, dx - 1)
    acc1_ref[...] = jnp.zeros(acc1_ref.shape, F32)
    acc2_ref[...] = jnp.zeros(acc2_ref.shape, F32)
    second = second_ref[...]

    def one_slice(hidden_slice, carry):
        kept = pl.ds(pl.multiple_of(hidden_slice * height, height), height)
        sum1 = None
        sum2 = None
        for tile in range(X // TILE):
            cols = slice(tile * TILE, (tile + 1) * TILE)
            high, low = patch(shifted_ref, hidden_slice, tile)
            g_high, g_low = patch(grad_ref, hidden_slice, tile)
            hidden = hidden_ref[kept, cols]
            grad_hidden = apply_spread(second, g_high, g_low)
            grad_pre = jnp.where(hidden.astype(F32) > 0.0, grad_hidden, 0.0).astype(BF16)
            part1 = dot_nt(grad_pre, padded_rows(high, low))
            part2 = dot_nt(hidden, padded_rows(g_high, g_low))
            sum1 = part1 if sum1 is None else sum1 + part1
            sum2 = part2 if sum2 is None else sum2 + part2
        acc1_ref[...] += sum1
        acc2_ref[...] += sum2
        return carry

    lax.fori_loop(0, hidden_count, one_slice, 0)

    def folded(ref):
        return ref[:, 0:LANES] + ref[:, LANES : 2 * LANES]

    total = gather_taps(
        ((folded(acc1_ref), first_column, True), (folded(acc2_ref), second_column, False)), channels
    )
    lane = iota((channels, LANES), 1)
    diagonal = lane == iota((channels, LANES), 0)
    line = jnp.sum(jnp.where(diagonal, total[:, TAPS : TAPS + 1], 0.0), axis=0, keepdims=True)
    line = jnp.where(lane[0:8] == LOSS_AT, loss, jnp.broadcast_to(line, (8, LANES)))
    out_ref[0:channels, :] = total
    out_ref[channels : channels + 8, :] = jnp.where(lane[0:8] == GRAD_B_SECOND_AT, grad_b2, line)


def backward(shifted, hidden, pred, parts, second, cells):
    height = second.shape[0]
    return pl.pallas_call(
        functools.partial(backward_kernel, cells, len(parts) // 2),
        out_shape=(
            jax.ShapeDtypeStruct((height // Y + 8, LANES), F32),
            jax.ShapeDtypeStruct(pred.shape, F32),
        ),
        in_specs=[VMEM] * (4 + len(parts)),
        out_specs=(VMEM, VMEM),
        scratch_shapes=[
            pltpu.VMEM(shifted.shape, F32),
            pltpu.VMEM((height, 2 * LANES), F32),
            pltpu.VMEM((height, 2 * LANES), F32),
        ],
        compiler_params=vmem_mib(18),
        name="backward",
    )(shifted, hidden, pred, second, *parts)


def finish_kernel(one_ref, two_ref, loss_ref, w1_ref, b1_ref, w2_ref, b2_ref):
    total = one_ref[...] + two_ref[...]
    channels = w1_ref.shape[0]
    line = total[channels : channels + 1]
    loss_ref[...] = line[:, LOSS_AT : LOSS_AT + 1]
    w1_ref[...] = total[0:channels, 0:TAPS]
    b1_ref[...] = line[:, 0:channels]
    w2_ref[...] = total[0:channels, W_SECOND_AT : W_SECOND_AT + TAPS]
    b2_ref[...] = line[:, GRAD_B_SECOND_AT : GRAD_B_SECOND_AT + 1]


def sum_everywhere(value, channels):
    devices = lax.axis_size("subset") * lax.axis_size("slab")
    apart = 1
    while True:
        arrived = lax.ppermute(value, BOTH, [(i, i ^ apart) for i in range(devices)])
        apart *= 2
        if apart == devices:
            break
        value = value + arrived
    shapes = ((1, 1), (channels, TAPS), (1, channels), (channels, TAPS), (1, 1))
    return pl.pallas_call(
        finish_kernel,
        out_shape=tuple(jax.ShapeDtypeStruct(shape, F32) for shape in shapes),
        in_specs=[VMEM, VMEM],
        out_specs=(VMEM,) * 5,
        compiler_params=vmem_mib(1),
        name="finish",
    )(value, arrived)


def body(sinogram, angles, w_first, b_first, w_second, b_second):
    n_sub = lax.axis_size("subset") // 2
    n_slab = lax.axis_size("slab")
    devices = 2 * n_sub * n_slab
    group = 2 * n_slab
    local_views, z_count = sinogram.shape[0], sinogram.shape[1]
    depth = z_count // group
    channels = w_first.shape[0]
    scale = math.pi / (local_views * group)
    cells = float(n_sub * z_count * Y * X)
    assert devices & (devices - 1) == 0 and n_slab > 1 and channels == 32 and depth >= HALO

    sent = pack(angles, sinogram, n_slab, depth)

    def exchange(value, distance):
        return lax.ppermute(value, BOTH, [(i, i ^ distance) for i in range(devices)])

    arrived = [sent[0]] + [None] * (n_slab - 1)
    for distance in range(1, n_slab):
        arrived[distance] = exchange(sent[distance], distance)
    near = n_slab // 2
    sums = project(arrived[:near], (), 0.0)
    sums, w_first, b_first, w_second, b_second = lax.optimization_barrier(
        (sums, w_first, b_first, w_second, b_second)
    )
    params = jnp.concatenate(
        [
            w_first,
            b_first[:, None],
            jnp.zeros((channels, W_SECOND_AT - TAPS - 1), F32),
            w_second,
            jnp.broadcast_to(b_second, (channels, LANES - W_SECOND_AT - TAPS)),
        ],
        axis=1,
    )
    sums, (first, second, turned) = lax.optimization_barrier((sums, weights(params)))
    mine, other, own, away = project(arrived[near:], sums[:2], scale)
    came = exchange(other, n_slab)
    parts = []
    for apart in range(1, n_sub):
        straight = [(i, (i + apart * group) % devices) for i in range(devices)]
        crossed = [(i, j ^ n_slab) for i, j in straight]
        parts.append(lax.ppermute(own, BOTH, straight))
        parts.append(lax.ppermute(away, BOTH, crossed))

    pred, again, shifted, hidden = forward(mine, came, params, first, turned)
    partial, target = backward(shifted, hidden, again, parts, second, cells)
    loss, grad_w1, grad_b1, grad_w2, grad_b2 = sum_everywhere(partial, channels)
    return (
        pred[None],
        target[None],
        loss.reshape(()),
        grad_w1,
        grad_b1.reshape(-1),
        grad_w2,
        grad_b2.reshape(-1),
    )


def solution(mesh):
    return jax.shard_map(
        body,
        mesh=mesh,
        in_specs=(P(BOTH, None, None), P(BOTH), P(), P(), P(), P()),
        out_specs=(
            P("subset", "slab", None, None),
            P("subset", "slab", None, None),
            P(),
            P(),
            P(),
            P(),
            P(),
        ),
        check_vma=False,
    )
```

```python
import functools
import math

import jax
import jax.numpy as jnp
from jax import lax
from jax.experimental import pallas as pl
from jax.experimental.pallas import tpu as pltpu
from jax.sharding import PartitionSpec as P


DET = 2048
X = 1024
Y = 8
LANES = 128
TAPS = 27
TILE = 256
BLOCK = 80
W_SECOND_AT = 32
B_SECOND_AT = 59
LOSS_AT = 64
GRAD_B_SECOND_AT = 65
HALO = 2
BOTH = ("subset", "slab")

RADIUS = math.hypot((X - 1) / 2.0, (Y - 1) / 2.0) + 0.25
FIRST_D = math.floor((DET - 1) / 2.0 - RADIUS)
LAST_D = math.floor((DET - 1) / 2.0 + RADIUS) + 1
D0 = FIRST_D - 8
DW = -(-(LAST_D + 1 - D0) // LANES) * LANES
READ_D = D0 // LANES * LANES
READ_W = -(-(D0 + DW - READ_D) // LANES) * LANES
assert D0 >= 0 and READ_D + READ_W <= DET

F32 = jnp.float32
BF16 = jnp.bfloat16
VMEM = pl.BlockSpec(memory_space=pltpu.VMEM)
SMEM = pl.BlockSpec(memory_space=pltpu.SMEM)


def vmem_mib(count):
    return pltpu.CompilerParams(vmem_limit_bytes=count * 2**20)


def iota(shape, dim):
    return lax.broadcasted_iota(jnp.int32, shape, dim)


def split2(value):
    high = value.astype(BF16)
    return high, (value - high.astype(F32)).astype(BF16)


def dot(a, b):
    return jnp.dot(a, b, preferred_element_type=F32)


def dot_nt(a, b):
    return lax.dot_general(a, b, (((1,), (1,)), ((), ())), preferred_element_type=F32)


def pack_kernel(depth, angle_ref, sino_ref, *refs):
    out_refs, (held_ref, rows_ref, cut_ref, sems) = refs[:-4], refs[-4:]
    views, z_count = sino_ref.shape[0], sino_ref.shape[1]
    n_slab = len(out_refs)
    rows = depth + 2 * HALO
    half = lax.axis_index("subset") % 2
    slab = lax.axis_index("slab")
    copies = [
        pltpu.make_async_copy(
            sino_ref.at[view, :, pl.ds(READ_D, READ_W)], held_ref.at[view], sems.at[view]
        )
        for view in range(views)
    ]
    for copy in copies:
        copy.start()
    lane = iota((rows, LANES), 1)
    zeros = jnp.zeros((8, DW), F32)
    rows_ref[0:8, :] = zeros
    rows_ref[8 + z_count : 16 + z_count, :] = zeros
    for view in range(views):
        angle = jnp.full((rows, LANES), angle_ref[view], F32)
        head = jnp.zeros((rows, LANES), F32)
        for which, left in enumerate((jnp.cos(angle), jnp.sin(angle))):
            for part in range(3):
                piece = left.astype(BF16).astype(F32)
                left = left - piece
                head = jnp.where(lane == 3 * which + part, piece, head)
        copies[view].wait()
        moved = pltpu.roll(held_ref[view].astype(F32), (READ_D - D0) % READ_W, 1)
        rows_ref[8 : 8 + z_count, :] = moved[:, 0:DW]
        for to in range(2 * n_slab):
            start = 8 + to * depth - HALO
            cut_ref[to] = rows_ref[start : start + rows, :]
            first = rows_ref[start : start + rows, 0:LANES]
            cut_ref[to, :, 0:LANES] = jnp.where(lane < 6, head, first)
        for apart, out_ref in enumerate(out_refs):
            to = jnp.bitwise_xor(slab, apart)
            mine = cut_ref[half * n_slab + to]
            other = cut_ref[(1 - half) * n_slab + to]
            out_ref[view] = jnp.concatenate([mine, other], axis=0).astype(BF16)


def pack(angles, sino, n_slab, depth):
    views, z_count = sino.shape[0], sino.shape[1]
    rows = depth + 2 * HALO
    return pl.pallas_call(
        functools.partial(pack_kernel, depth),
        out_shape=(jax.ShapeDtypeStruct((views, 2 * rows, DW), BF16),) * n_slab,
        in_specs=[SMEM, pl.BlockSpec(memory_space=pltpu.HBM)],
        out_specs=(VMEM,) * n_slab,
        scratch_shapes=[
            pltpu.VMEM((views, z_count, READ_W), BF16),
            pltpu.VMEM((z_count + 16, DW), F32),
            pltpu.VMEM((2 * n_slab, rows, DW), F32),
            pltpu.SemaphoreType.DMA((views,)),
        ],
        compiler_params=vmem_mib(8),
        name="pack",
    )(
        pltpu.with_memory_space_constraint(angles, pltpu.HBM),
        pltpu.with_memory_space_constraint(sino, pltpu.HBM),
    )


def project_kernel(count, scale, *refs):
    data_refs = refs[:count]
    init_refs = refs[count:-7]
    mine_ref, other_ref, low_ref, high_ref, tab_ref, scal_ref, sem = refs[-7:]
    each = data_refs[0].shape[0]
    views, rows = count * each, data_refs[0].shape[1]
    window = rows // 2
    centre = (DET - 1) / 2.0
    for place, data_ref in enumerate(data_refs):
        values = data_ref[...].astype(F32)
        moved = pltpu.roll(values.reshape(each * rows, DW), DW - 1, 1).reshape(values.shape)
        here = slice(place * each, (place + 1) * each)
        for tile in range(DW // LANES):
            cols = slice(tile * LANES, (tile + 1) * LANES)
            low_ref[here, tile] = values[:, :, cols]
            high_ref[here, tile] = moved[:, :, cols]
    head = low_ref[:, 0, 0, :]
    cosine = jnp.broadcast_to(head[:, 0:1] + head[:, 1:2] + head[:, 2:3], (views, LANES))
    sine = jnp.broadcast_to(head[:, 3:4] + head[:, 4:5] + head[:, 5:6], (views, LANES))

    def at(col, row):
        return col * cosine + row * sine + centre

    start = (iota((views, LANES), 1) % (X // LANES)).astype(F32) * LANES - (X - 1) / 2.0
    stop = start + (LANES - 1.0)
    edge = (Y - 1) / 2.0
    least = jnp.minimum(
        jnp.minimum(at(start, -edge), at(stop, -edge)), jnp.minimum(at(start, edge), at(stop, edge))
    )
    tab_ref[0] = cosine
    tab_ref[1] = sine
    tab_ref[2] = ((jnp.floor(least).astype(jnp.int32) - D0) // LANES).astype(F32)
    copy = pltpu.make_async_copy(tab_ref, scal_ref, sem)
    copy.start()
    copy.wait()

    lane = iota((views, LANES), 1)
    row_of_lane = (lane // (X // LANES) % Y).astype(F32) - edge
    ends = jnp.floor(at(stop, row_of_lane)) - jnp.floor(at(start, row_of_lane))
    apart = jnp.max(jnp.abs(ends)) >= float(LANES)

    lanes = iota((Y, LANES), 1)
    column = lanes.astype(F32)
    row_pos = iota((Y, LANES), 0).astype(F32) - edge

    def all_blocks(distinct):
        def one_block(block, carry):
            left = block.astype(F32) * LANES - (X - 1) / 2.0
            col = column + left

            def one_view(view, sums):
                tile = scal_ref[2, view, block].astype(jnp.int32)
                cos_part = scal_ref[0, view, 0]
                sin_part = row_pos * scal_ref[1, view, 0]
                position = col * cos_part + sin_part + centre
                lower = jnp.floor(position)
                weight_low = jnp.maximum(0.0, 1.0 - jnp.abs(position - lower))
                weight_high = jnp.maximum(0.0, 1.0 - jnp.abs(position - (lower + 1.0)))
                weight_low = weight_low.astype(BF16).astype(F32)
                weight_high = weight_high.astype(BF16).astype(F32)
                base = D0 + tile * LANES
                index = lower.astype(jnp.int32) - base
                second = index >= LANES
                index = jnp.bitwise_and(index, LANES - 1)
                if distinct:
                    end1 = left * cos_part + sin_part + centre
                    end2 = (left + (LANES - 1.0)) * cos_part + sin_part + centre
                    least_index = jnp.floor(jnp.minimum(end1, end2)).astype(jnp.int32) - base
                    in_first = lanes >= least_index

                def take(ref, z):
                    def line(at_tile):
                        return ref[view, at_tile, pl.ds(z, Y, stride=0), :]

                    def pick(values):
                        return jnp.take_along_axis(
                            values, index, axis=1, mode="promise_in_bounds"
                        )

                    one, two = line(tile), line(tile + 1)
                    if distinct:
                        return pick(jnp.where(in_first, one, two))
                    return jnp.where(second, pick(two), pick(one))

                return tuple(
                    sums[z] + (weight_low * take(low_ref, z) + weight_high * take(high_ref, z))
                    for z in range(rows)
                )

            cols = pl.ds(pl.multiple_of(block * LANES, LANES), LANES)
            if init_refs:
                sums = tuple(
                    init_refs[z // window][z % window, :, cols] for z in range(rows)
                )
            else:
                sums = tuple(jnp.zeros((Y, LANES), F32) for _ in range(rows))
            sums = lax.fori_loop(0, views, one_view, sums, unroll=views if distinct else 1)
            for z in range(rows):
                done = sums[z] * scale if scale else sums[z]
                (mine_ref, other_ref)[z // window][z % window, :, cols] = done
            return carry

        lax.fori_loop(0, X // LANES, one_block, 0)

    pl.when(apart)(lambda: all_blocks(False))
    pl.when(jnp.logical_not(apart))(lambda: all_blocks(True))


def project(chunks, init, scale):
    count = len(chunks)
    views, rows = count * chunks[0].shape[0], chunks[0].shape[1]
    whole = jax.ShapeDtypeStruct((rows // 2, Y, X), F32)
    return pl.pallas_call(
        functools.partial(project_kernel, count, scale),
        out_shape=(whole, whole),
        in_specs=[VMEM] * (count + len(init)),
        out_specs=(VMEM, VMEM),
        scratch_shapes=[
            pltpu.VMEM((views, DW // LANES, rows, LANES), F32),
            pltpu.VMEM((views, DW // LANES, rows, LANES), F32),
            pltpu.VMEM((3, views, LANES), F32),
            pltpu.SMEM((3, views, LANES), F32),
            pltpu.SemaphoreType.DMA,
        ],
        compiler_params=vmem_mib(14),
        cost_estimate=pl.CostEstimate(
            flops=4_000_000_000, bytes_accessed=1_500_000, transcendentals=0
        ),
        name="project",
    )(*chunks, *init)


def first_column(dx, dz, dy):
    return 9 * dz + 3 * dy + dx


def second_column(dx, dz, dy):
    return W_SECOND_AT + (TAPS - 1) - first_column(dx, dz, dy)


def spread(params, column_of, bias):
    channels = params.shape[0]
    height = channels * Y
    high, low = split2(params)
    both = jnp.concatenate([high, low], axis=1)
    rep = (iota((height, channels), 0) // Y == iota((height, channels), 1)).astype(F32)
    rep = rep.astype(BF16)
    shape = (2 * LANES, TILE)
    source = iota(shape, 0)
    col = iota(shape, 1)
    part, inner = col // BLOCK, col % BLOCK
    wanted_half = jnp.where(part == 2, 1, 0)
    usable = (part < 3) & (source // LANES == wanted_half)
    out_col = iota((height, TILE), 1)
    out_inner = out_col % BLOCK
    out_y = iota((height, TILE), 0) % Y
    total = jnp.zeros((height, TILE), F32)
    for dy in range(3):
        wanted = column_of(inner // 24, (inner // 8) % 3, dy)
        pick = usable & (inner < 72) & (source % LANES == wanted)
        if bias and dy == 1:
            pick = pick | (usable & (inner == 72) & (source % LANES == TAPS))
        chosen = dot(both, pick.astype(F32).astype(BF16)).astype(BF16)
        here = (out_inner < 72) & (out_inner % 8 - out_y + 1 == dy)
        if bias and dy == 1:
            here = here | (out_inner == 72)
        total = total + jnp.where(here, dot(rep, chosen), 0.0)
    return total.astype(BF16)


def gather_taps(grads, channels):
    height = channels * Y
    col = iota((height, LANES), 1)
    row_y = iota((height, LANES), 0) % Y
    inner = iota((LANES, LANES), 0)
    to = iota((LANES, LANES), 1)
    pieces = []
    picks = []
    for grad, column_of, bias in grads:
        for dy in range(3):
            here = (col < 72) & (col % 8 - row_y + 1 == dy)
            pick = (inner < 72) & (to == column_of(inner // 24, (inner // 8) % 3, dy))
            if bias and dy == 1:
                here = here | (col == 72)
                pick = pick | ((inner == 72) & (to == TAPS))
            masked = jnp.where(here, grad, 0.0).reshape(channels, Y, LANES)
            pieces.append(jnp.sum(masked, axis=1))
            picks.append(pick.astype(F32))
    return jnp.dot(
        jnp.concatenate(pieces, axis=1),
        jnp.concatenate(picks, axis=0),
        precision=lax.Precision.HIGHEST,
        preferred_element_type=F32,
    )


def shift_columns(value, by):
    if by == 0:
        return value
    rolled = pltpu.roll(value, (-by) % X, 1)
    lane = iota(value.shape, 1)
    return jnp.where(lane == (X - 1 if by > 0 else 0), 0.0, rolled)


def fill_shifted(ref, field):
    for dx in range(3):
        ref[dx] = shift_columns(field, dx - 1)


def patch(ref, slice_index, tile):
    at = pl.multiple_of(slice_index * Y, Y)
    cols = slice(tile * TILE, (tile + 1) * TILE)
    pieces = [ref[dx, pl.ds(at, 3 * Y), cols] for dx in range(3)]
    pieces.append((iota((8, TILE), 0) == 0).astype(F32))
    high, low = split2(jnp.concatenate(pieces, axis=0))
    return high, low


def apply_spread(weights, high, low):
    return dot(weights[:, 0 : 3 * BLOCK], jnp.concatenate([high, low, high], axis=0))


def slice_flag(hidden_slice, hidden_count):
    n_slab = lax.axis_size("slab")
    place = (lax.axis_index("subset") % 2) * n_slab + lax.axis_index("slab")
    outside = ((hidden_slice == 0) & (place == 0)) | (
        (hidden_slice == hidden_count - 1) & (place == 2 * n_slab - 1)
    )
    return jnp.where(outside, 0.0, 1.0).astype(F32)


def weights_kernel(params_ref, first_ref, second_ref, turned_ref):
    params = params_ref[...]
    second = spread(params, second_column, False)
    first_ref[...] = spread(params, first_column, True)
    second_ref[...] = second
    turned_ref[...] = second.astype(F32).T.astype(BF16)


def weights(params):
    height = params.shape[0] * Y
    return pl.pallas_call(
        weights_kernel,
        out_shape=(
            jax.ShapeDtypeStruct((height, TILE), BF16),
            jax.ShapeDtypeStruct((height, TILE), BF16),
            jax.ShapeDtypeStruct((TILE, height), BF16),
        ),
        in_specs=[VMEM],
        out_specs=(VMEM,) * 3,
        compiler_params=vmem_mib(8),
        name="weights",
    )(params)


def join_kernel(mine_ref, came_ref, own_ref, shifted_ref):
    rows = mine_ref.shape[0]
    both = mine_ref[...] + came_ref[...]
    own_ref[...] = both[HALO : rows - HALO]
    fill_shifted(shifted_ref, both.reshape(rows * Y, X))


def join(mine, came):
    rows = mine.shape[0]
    return pl.pallas_call(
        join_kernel,
        out_shape=(
            jax.ShapeDtypeStruct((rows - 2 * HALO, Y, X), F32),
            jax.ShapeDtypeStruct((3, rows * Y, X), F32),
        ),
        in_specs=[VMEM] * 2,
        out_specs=(VMEM,) * 2,
        compiler_params=vmem_mib(8),
        name="join",
    )(mine, came)


def forward_kernel(
    shifted_ref, params_ref, first_ref, turned_ref, pred_ref, again_ref, hidden_ref, acc_ref
):
    rows = shifted_ref.shape[1] // Y
    hidden_count = rows - 2
    height = first_ref.shape[0]
    first = first_ref[...]
    acc_ref[...] = jnp.zeros(acc_ref.shape, F32)

    def one_slice(hidden_slice, carry):
        flag = slice_flag(hidden_slice, hidden_count)
        at = pl.multiple_of(hidden_slice * Y, Y)
        kept = pl.ds(pl.multiple_of(hidden_slice * height, height), height)
        for tile in range(X // TILE):
            cols = slice(tile * TILE, (tile + 1) * TILE)
            high, low = patch(shifted_ref, hidden_slice, tile)
            hidden = jnp.maximum(apply_spread(first, high, low), 0.0) * flag
            h_high, h_low = split2(hidden)
            hidden_ref[kept, cols] = h_high
            main = dot(turned_ref[BLOCK : 3 * BLOCK], h_high)
            taps = main[0:BLOCK] + main[BLOCK : 2 * BLOCK] + dot(turned_ref[0:BLOCK], h_low)
            for dx in range(3):
                acc_ref[dx, pl.ds(at, 3 * Y), cols] += taps[24 * dx : 24 * dx + 24]
        return carry

    lax.fori_loop(0, hidden_count, one_slice, 0)
    inner = slice(HALO * Y, (rows - HALO) * Y)
    added = acc_ref[1, inner, :]
    for dx in (0, 2):
        added = added + shift_columns(acc_ref[dx, inner, :], 1 - dx)
    own = shifted_ref[1, inner, :]
    bias = params_ref[0:1, B_SECOND_AT : B_SECOND_AT + 1]
    pred = (own + added + bias).reshape(pred_ref.shape)
    pred_ref[...] = pred
    again_ref[...] = pred


def forward(shifted, params, first, turned):
    rows = shifted.shape[1] // Y
    height = first.shape[0]
    own = jax.ShapeDtypeStruct((rows - 2 * HALO, Y, X), F32)
    return pl.pallas_call(
        forward_kernel,
        out_shape=(
            own,
            own,
            jax.ShapeDtypeStruct(((rows - 2) * height, X), BF16),
        ),
        in_specs=[VMEM] * 4,
        out_specs=(VMEM,) * 3,
        scratch_shapes=[pltpu.VMEM((3, rows * Y, X), F32)],
        cost_estimate=pl.CostEstimate(
            flops=20_000_000_000, bytes_accessed=2_000_000, transcendentals=0
        ),
        compiler_params=vmem_mib(18),
        name="forward",
    )(shifted, params, first, turned)


def padded_rows(high, low):
    none = jnp.zeros((LANES - BLOCK, high.shape[1]), BF16)
    return jnp.concatenate([high, none, low, none], axis=0)


def backward_kernel(cells, others, shifted_ref, hidden_ref, pred_ref, second_ref, *refs):
    part_refs = refs[:others]
    out_ref, target_out_ref, grad_ref, acc1_ref, acc2_ref = refs[others:]
    rows = shifted_ref.shape[1] // Y
    hidden_count = rows - 2
    height = second_ref.shape[0]
    channels = height // Y
    target = part_refs[0][...]
    for part_ref in part_refs[1:]:
        target = target + part_ref[...]
    target = target if others == 1 else target / others
    target_out_ref[...] = target
    diff = (pred_ref[...] - target).reshape((rows - 2 * HALO) * Y, X)
    resid = 2.0 * diff / cells
    loss = jnp.sum(diff * diff, keepdims=True) / cells
    grad_b2 = jnp.sum(resid, keepdims=True)
    inner = slice(HALO * Y, (rows - HALO) * Y)
    for dx in range(3):
        grad_ref[dx, 0 : HALO * Y, :] = jnp.zeros((HALO * Y, X), F32)
        grad_ref[dx, (rows - HALO) * Y : rows * Y, :] = jnp.zeros((HALO * Y, X), F32)
        grad_ref[dx, inner, :] = shift_columns(resid, dx - 1)
    acc1_ref[...] = jnp.zeros(acc1_ref.shape, F32)
    acc2_ref[...] = jnp.zeros(acc2_ref.shape, F32)
    second = second_ref[...]

    def one_slice(hidden_slice, carry):
        kept = pl.ds(pl.multiple_of(hidden_slice * height, height), height)
        sum1 = None
        sum2 = None
        for tile in range(X // TILE):
            cols = slice(tile * TILE, (tile + 1) * TILE)
            high, low = patch(shifted_ref, hidden_slice, tile)
            g_high, g_low = patch(grad_ref, hidden_slice, tile)
            hidden = hidden_ref[kept, cols]
            grad_hidden = apply_spread(second, g_high, g_low)
            grad_pre = jnp.where(hidden.astype(F32) > 0.0, grad_hidden, 0.0).astype(BF16)
            part1 = dot_nt(grad_pre, padded_rows(high, low))
            part2 = dot_nt(hidden, padded_rows(g_high, g_low))
            sum1 = part1 if sum1 is None else sum1 + part1
            sum2 = part2 if sum2 is None else sum2 + part2
        acc1_ref[...] += sum1
        acc2_ref[...] += sum2
        return carry

    lax.fori_loop(0, hidden_count, one_slice, 0)

    def folded(ref):
        return ref[:, 0:LANES] + ref[:, LANES : 2 * LANES]

    total = gather_taps(
        ((folded(acc1_ref), first_column, True), (folded(acc2_ref), second_column, False)), channels
    )
    lane = iota((channels, LANES), 1)
    diagonal = lane == iota((channels, LANES), 0)
    line = jnp.sum(jnp.where(diagonal, total[:, TAPS : TAPS + 1], 0.0), axis=0, keepdims=True)
    line = jnp.where(lane[0:8] == LOSS_AT, loss, jnp.broadcast_to(line, (8, LANES)))
    out_ref[0:channels, :] = total
    out_ref[channels : channels + 8, :] = jnp.where(lane[0:8] == GRAD_B_SECOND_AT, grad_b2, line)


def backward(shifted, hidden, pred, parts, second, cells):
    height = second.shape[0]
    return pl.pallas_call(
        functools.partial(backward_kernel, cells, len(parts)),
        out_shape=(
            jax.ShapeDtypeStruct((height // Y + 8, LANES), F32),
            jax.ShapeDtypeStruct(pred.shape, F32),
        ),
        in_specs=[VMEM] * (4 + len(parts)),
        out_specs=(VMEM, VMEM),
        scratch_shapes=[
            pltpu.VMEM(shifted.shape, F32),
            pltpu.VMEM((height, 2 * LANES), F32),
            pltpu.VMEM((height, 2 * LANES), F32),
        ],
        compiler_params=vmem_mib(18),
        name="backward",
    )(shifted, hidden, pred, second, *parts)


def finish_kernel(one_ref, two_ref, loss_ref, w1_ref, b1_ref, w2_ref, b2_ref):
    total = one_ref[...] + two_ref[...]
    channels = w1_ref.shape[0]
    line = total[channels : channels + 1]
    loss_ref[...] = line[:, LOSS_AT : LOSS_AT + 1]
    w1_ref[...] = total[0:channels, 0:TAPS]
    b1_ref[...] = line[:, 0:channels]
    w2_ref[...] = total[0:channels, W_SECOND_AT : W_SECOND_AT + TAPS]
    b2_ref[...] = line[:, GRAD_B_SECOND_AT : GRAD_B_SECOND_AT + 1]


def sum_everywhere(value, channels):
    devices = lax.axis_size("subset") * lax.axis_size("slab")
    apart = 1
    while True:
        arrived = lax.ppermute(value, BOTH, [(i, i ^ apart) for i in range(devices)])
        apart *= 2
        if apart == devices:
            break
        value = value + arrived
    shapes = ((1, 1), (channels, TAPS), (1, channels), (channels, TAPS), (1, 1))
    return pl.pallas_call(
        finish_kernel,
        out_shape=tuple(jax.ShapeDtypeStruct(shape, F32) for shape in shapes),
        in_specs=[VMEM, VMEM],
        out_specs=(VMEM,) * 5,
        compiler_params=vmem_mib(1),
        name="finish",
    )(value, arrived)


def body(sinogram, angles, w_first, b_first, w_second, b_second):
    n_sub = lax.axis_size("subset") // 2
    n_slab = lax.axis_size("slab")
    devices = 2 * n_sub * n_slab
    group = 2 * n_slab
    local_views, z_count = sinogram.shape[0], sinogram.shape[1]
    depth = z_count // group
    channels = w_first.shape[0]
    scale = math.pi / (local_views * group)
    cells = float(n_sub * z_count * Y * X)
    assert devices & (devices - 1) == 0 and n_slab > 1 and channels == 32 and depth >= HALO

    sent = pack(angles, sinogram, n_slab, depth)

    def exchange(value, distance):
        return lax.ppermute(value, BOTH, [(i, i ^ distance) for i in range(devices)])

    arrived = [sent[0]] + [None] * (n_slab - 1)
    for distance in range(1, n_slab):
        arrived[distance] = exchange(sent[distance], distance)
    near = n_slab // 2 + 1
    sums = project(arrived[:near], (), 0.0)
    sums, w_first, b_first, w_second, b_second = lax.optimization_barrier(
        (sums, w_first, b_first, w_second, b_second)
    )
    params = jnp.concatenate(
        [
            w_first,
            b_first[:, None],
            jnp.zeros((channels, W_SECOND_AT - TAPS - 1), F32),
            w_second,
            jnp.broadcast_to(b_second, (channels, LANES - W_SECOND_AT - TAPS)),
        ],
        axis=1,
    )
    sums, (first, second, turned) = lax.optimization_barrier((sums, weights(params)))
    mine, other = project(arrived[near:], sums, scale)
    came = exchange(other, n_slab)
    own, shifted = join(mine, came)
    parts = []
    for apart in range(1, n_sub):
        pairs = [(i, (i + apart * group) % devices) for i in range(devices)]
        parts.append(lax.ppermute(own, BOTH, pairs))

    pred, again, hidden = forward(shifted, params, first, turned)
    partial, target = backward(shifted, hidden, again, parts, second, cells)
    loss, grad_w1, grad_b1, grad_w2, grad_b2 = sum_everywhere(partial, channels)
    return (
        pred[None],
        target[None],
        loss.reshape(()),
        grad_w1,
        grad_b1.reshape(-1),
        grad_w2,
        grad_b2.reshape(-1),
    )


def solution(mesh):
    return jax.shard_map(
        body,
        mesh=mesh,
        in_specs=(P(BOTH, None, None), P(BOTH), P(), P(), P(), P()),
        out_specs=(
            P("subset", "slab", None, None),
            P("subset", "slab", None, None),
            P(),
            P(),
            P(),
            P(),
            P(),
        ),
        check_vma=False,
    )
```

```python
import functools
import math

import jax
import jax.numpy as jnp
from jax import lax
from jax.experimental import pallas as pl
from jax.experimental.pallas import tpu as pltpu
from jax.sharding import PartitionSpec as P


DET = 2048
X = 1024
Y = 8
LANES = 128
TAPS = 27
TILE = 256
BLOCK = 80
W_SECOND_AT = 32
B_SECOND_AT = 59
LOSS_AT = 64
GRAD_B_SECOND_AT = 65
HALO = 2
BOTH = ("subset", "slab")

RADIUS = math.hypot((X - 1) / 2.0, (Y - 1) / 2.0) + 0.25
FIRST_D = math.floor((DET - 1) / 2.0 - RADIUS)
LAST_D = math.floor((DET - 1) / 2.0 + RADIUS) + 1
D0 = FIRST_D - 8
DW = -(-(LAST_D + 1 - D0) // LANES) * LANES
READ_D = D0 // LANES * LANES
READ_W = -(-(D0 + DW - READ_D) // LANES) * LANES
assert D0 >= 0 and READ_D + READ_W <= DET

F32 = jnp.float32
BF16 = jnp.bfloat16
VMEM = pl.BlockSpec(memory_space=pltpu.VMEM)
SMEM = pl.BlockSpec(memory_space=pltpu.SMEM)


def vmem_mib(count):
    return pltpu.CompilerParams(vmem_limit_bytes=count * 2**20)


def iota(shape, dim):
    return lax.broadcasted_iota(jnp.int32, shape, dim)


def split2(value):
    high = value.astype(BF16)
    return high, (value - high.astype(F32)).astype(BF16)


def dot(a, b):
    return jnp.dot(a, b, preferred_element_type=F32)


def dot_nt(a, b):
    return lax.dot_general(a, b, (((1,), (1,)), ((), ())), preferred_element_type=F32)


def pack_kernel(depth, angle_ref, sino_ref, *refs):
    out_refs, (held_ref, rows_ref, cut_ref, sems) = refs[:-4], refs[-4:]
    views, z_count = sino_ref.shape[0], sino_ref.shape[1]
    n_slab = len(out_refs)
    rows = depth + 2 * HALO
    half = lax.axis_index("subset") % 2
    slab = lax.axis_index("slab")
    copies = [
        pltpu.make_async_copy(
            sino_ref.at[view, :, pl.ds(READ_D, READ_W)], held_ref.at[view], sems.at[view]
        )
        for view in range(views)
    ]
    for copy in copies:
        copy.start()
    lane = iota((rows, LANES), 1)
    zeros = jnp.zeros((8, DW), F32)
    rows_ref[0:8, :] = zeros
    rows_ref[8 + z_count : 16 + z_count, :] = zeros
    heads = []
    for view in range(views):
        angle = jnp.full((rows, LANES), angle_ref[view], F32)
        head = jnp.zeros((rows, LANES), F32)
        for which, left in enumerate((jnp.cos(angle), jnp.sin(angle))):
            for part in range(3):
                piece = left.astype(BF16).astype(F32)
                left = left - piece
                head = jnp.where(lane == 3 * which + part, piece, head)
        heads.append(head)
    for view in range(views):
        head = heads[view]
        copies[view].wait()
        moved = pltpu.roll(held_ref[view].astype(F32), (READ_D - D0) % READ_W, 1)
        rows_ref[8 : 8 + z_count, :] = moved[:, 0:DW]
        for to in range(2 * n_slab):
            start = 8 + to * depth - HALO
            cut_ref[to, :, LANES:DW] = rows_ref[start : start + rows, LANES:DW]
            first = rows_ref[start : start + rows, 0:LANES]
            cut_ref[to, :, 0:LANES] = jnp.where(lane < 6, head, first)
        for apart, out_ref in enumerate(out_refs):
            to = jnp.bitwise_xor(slab, apart)
            mine = cut_ref[half * n_slab + to]
            other = cut_ref[(1 - half) * n_slab + to]
            out_ref[view] = jnp.concatenate([mine, other], axis=0).astype(BF16)


def pack(angles, sino, n_slab, depth):
    views, z_count = sino.shape[0], sino.shape[1]
    rows = depth + 2 * HALO
    return pl.pallas_call(
        functools.partial(pack_kernel, depth),
        out_shape=(jax.ShapeDtypeStruct((views, 2 * rows, DW), BF16),) * n_slab,
        in_specs=[SMEM, pl.BlockSpec(memory_space=pltpu.HBM)],
        out_specs=(VMEM,) * n_slab,
        scratch_shapes=[
            pltpu.VMEM((views, z_count, READ_W), BF16),
            pltpu.VMEM((z_count + 16, DW), F32),
            pltpu.VMEM((2 * n_slab, rows, DW), F32),
            pltpu.SemaphoreType.DMA((views,)),
        ],
        compiler_params=vmem_mib(8),
        name="pack",
    )(
        pltpu.with_memory_space_constraint(angles, pltpu.HBM),
        pltpu.with_memory_space_constraint(sino, pltpu.HBM),
    )


def project_kernel(count, scale, *refs):
    data_refs = refs[:count]
    init_refs = refs[count:-7]
    mine_ref, other_ref, low_ref, high_ref, tab_ref, scal_ref, sem = refs[-7:]
    each = data_refs[0].shape[0]
    views, rows = count * each, data_refs[0].shape[1]
    window = rows // 2
    centre = (DET - 1) / 2.0
    for place, data_ref in enumerate(data_refs):
        values = data_ref[...].astype(F32)
        moved = pltpu.roll(values.reshape(each * rows, DW), DW - 1, 1).reshape(values.shape)
        here = slice(place * each, (place + 1) * each)
        for tile in range(DW // LANES):
            cols = slice(tile * LANES, (tile + 1) * LANES)
            low_ref[here, tile] = values[:, :, cols]
            high_ref[here, tile] = moved[:, :, cols]
    head = low_ref[:, 0, 0, :]
    cosine = jnp.broadcast_to(head[:, 0:1] + head[:, 1:2] + head[:, 2:3], (views, LANES))
    sine = jnp.broadcast_to(head[:, 3:4] + head[:, 4:5] + head[:, 5:6], (views, LANES))

    def at(col, row):
        return col * cosine + row * sine + centre

    start = (iota((views, LANES), 1) % (X // LANES)).astype(F32) * LANES - (X - 1) / 2.0
    stop = start + (LANES - 1.0)
    edge = (Y - 1) / 2.0
    least = jnp.minimum(
        jnp.minimum(at(start, -edge), at(stop, -edge)), jnp.minimum(at(start, edge), at(stop, edge))
    )
    tab_ref[0] = cosine
    tab_ref[1] = sine
    tab_ref[2] = ((jnp.floor(least).astype(jnp.int32) - D0) // LANES).astype(F32)
    copy = pltpu.make_async_copy(tab_ref, scal_ref, sem)
    copy.start()
    copy.wait()

    lane = iota((views, LANES), 1)
    row_of_lane = (lane // (X // LANES) % Y).astype(F32) - edge
    ends = jnp.floor(at(stop, row_of_lane)) - jnp.floor(at(start, row_of_lane))
    apart = jnp.max(jnp.abs(ends)) >= float(LANES)

    lanes = iota((Y, LANES), 1)
    column = lanes.astype(F32)
    row_pos = iota((Y, LANES), 0).astype(F32) - edge

    def all_blocks(distinct):
        def one_block(block, carry):
            left = block.astype(F32) * LANES - (X - 1) / 2.0
            col = column + left

            def one_view(view, sums):
                tile = scal_ref[2, view, block].astype(jnp.int32)
                cos_part = scal_ref[0, view, 0]
                sin_part = row_pos * scal_ref[1, view, 0]
                position = col * cos_part + sin_part + centre
                lower = jnp.floor(position)
                weight_low = jnp.maximum(0.0, 1.0 - jnp.abs(position - lower))
                weight_high = jnp.maximum(0.0, 1.0 - jnp.abs(position - (lower + 1.0)))
                weight_low = weight_low.astype(BF16).astype(F32)
                weight_high = weight_high.astype(BF16).astype(F32)
                base = D0 + tile * LANES
                index = lower.astype(jnp.int32) - base
                second = index >= LANES
                index = jnp.bitwise_and(index, LANES - 1)
                if distinct:
                    end1 = left * cos_part + sin_part + centre
                    end2 = (left + (LANES - 1.0)) * cos_part + sin_part + centre
                    least_index = jnp.floor(jnp.minimum(end1, end2)).astype(jnp.int32) - base
                    in_first = lanes >= least_index

                def take(ref, z):
                    def line(at_tile):
                        return ref[view, at_tile, pl.ds(z, Y, stride=0), :]

                    def pick(values):
                        return jnp.take_along_axis(
                            values, index, axis=1, mode="promise_in_bounds"
                        )

                    one, two = line(tile), line(tile + 1)
                    if distinct:
                        return pick(jnp.where(in_first, one, two))
                    return jnp.where(second, pick(two), pick(one))

                return tuple(
                    sums[z] + (weight_low * take(low_ref, z) + weight_high * take(high_ref, z))
                    for z in range(rows)
                )

            cols = pl.ds(pl.multiple_of(block * LANES, LANES), LANES)
            if init_refs:
                sums = tuple(
                    init_refs[z // window][z % window, :, cols] for z in range(rows)
                )
            else:
                sums = tuple(jnp.zeros((Y, LANES), F32) for _ in range(rows))
            sums = lax.fori_loop(0, views, one_view, sums, unroll=views if distinct else 1)
            for z in range(rows):
                done = sums[z] * scale if scale else sums[z]
                (mine_ref, other_ref)[z // window][z % window, :, cols] = done
            return carry

        lax.fori_loop(0, X // LANES, one_block, 0)

    pl.when(apart)(lambda: all_blocks(False))
    pl.when(jnp.logical_not(apart))(lambda: all_blocks(True))


def project(chunks, init, scale):
    count = len(chunks)
    views, rows = count * chunks[0].shape[0], chunks[0].shape[1]
    whole = jax.ShapeDtypeStruct((rows // 2, Y, X), F32)
    return pl.pallas_call(
        functools.partial(project_kernel, count, scale),
        out_shape=(whole, whole),
        in_specs=[VMEM] * (count + len(init)),
        out_specs=(VMEM, VMEM),
        scratch_shapes=[
            pltpu.VMEM((views, DW // LANES, rows, LANES), F32),
            pltpu.VMEM((views, DW // LANES, rows, LANES), F32),
            pltpu.VMEM((3, views, LANES), F32),
            pltpu.SMEM((3, views, LANES), F32),
            pltpu.SemaphoreType.DMA,
        ],
        compiler_params=vmem_mib(14),
        cost_estimate=pl.CostEstimate(
            flops=4_000_000_000, bytes_accessed=1_500_000, transcendentals=0
        ),
        name="project",
    )(*chunks, *init)


def first_column(dx, dz, dy):
    return 9 * dz + 3 * dy + dx


def second_column(dx, dz, dy):
    return W_SECOND_AT + (TAPS - 1) - first_column(dx, dz, dy)


def spread(params, column_of, bias):
    channels = params.shape[0]
    height = channels * Y
    high, low = split2(params)
    both = jnp.concatenate([high, low], axis=1)
    rep = (iota((height, channels), 0) // Y == iota((height, channels), 1)).astype(F32)
    rep = rep.astype(BF16)
    shape = (2 * LANES, TILE)
    source = iota(shape, 0)
    col = iota(shape, 1)
    part, inner = col // BLOCK, col % BLOCK
    wanted_half = jnp.where(part == 2, 1, 0)
    usable = (part < 3) & (source // LANES == wanted_half)
    out_col = iota((height, TILE), 1)
    out_inner = out_col % BLOCK
    out_y = iota((height, TILE), 0) % Y
    total = jnp.zeros((height, TILE), F32)
    for dy in range(3):
        wanted = column_of(inner // 24, (inner // 8) % 3, dy)
        pick = usable & (inner < 72) & (source % LANES == wanted)
        if bias and dy == 1:
            pick = pick | (usable & (inner == 72) & (source % LANES == TAPS))
        chosen = dot(both, pick.astype(F32).astype(BF16)).astype(BF16)
        here = (out_inner < 72) & (out_inner % 8 - out_y + 1 == dy)
        if bias and dy == 1:
            here = here | (out_inner == 72)
        total = total + jnp.where(here, dot(rep, chosen), 0.0)
    return total.astype(BF16)


def gather_taps(grads, channels):
    height = channels * Y
    col = iota((height, LANES), 1)
    row_y = iota((height, LANES), 0) % Y
    inner = iota((LANES, LANES), 0)
    to = iota((LANES, LANES), 1)
    pieces = []
    picks = []
    for grad, column_of, bias in grads:
        for dy in range(3):
            here = (col < 72) & (col % 8 - row_y + 1 == dy)
            pick = (inner < 72) & (to == column_of(inner // 24, (inner // 8) % 3, dy))
            if bias and dy == 1:
                here = here | (col == 72)
                pick = pick | ((inner == 72) & (to == TAPS))
            masked = jnp.where(here, grad, 0.0).reshape(channels, Y, LANES)
            pieces.append(jnp.sum(masked, axis=1))
            picks.append(pick.astype(F32))
    return jnp.dot(
        jnp.concatenate(pieces, axis=1),
        jnp.concatenate(picks, axis=0),
        precision=lax.Precision.HIGHEST,
        preferred_element_type=F32,
    )


def shift_columns(value, by):
    if by == 0:
        return value
    rolled = pltpu.roll(value, (-by) % X, 1)
    lane = iota(value.shape, 1)
    return jnp.where(lane == (X - 1 if by > 0 else 0), 0.0, rolled)


def fill_shifted(ref, field):
    for dx in range(3):
        ref[dx] = shift_columns(field, dx - 1)


def patch(ref, slice_index, tile):
    at = pl.multiple_of(slice_index * Y, Y)
    cols = slice(tile * TILE, (tile + 1) * TILE)
    pieces = [ref[dx, pl.ds(at, 3 * Y), cols] for dx in range(3)]
    pieces.append((iota((8, TILE), 0) == 0).astype(F32))
    high, low = split2(jnp.concatenate(pieces, axis=0))
    return high, low


def apply_spread(weights, high, low):
    return dot(weights[:, 0 : 3 * BLOCK], jnp.concatenate([high, low, high], axis=0))


def slice_flag(hidden_slice, hidden_count):
    n_slab = lax.axis_size("slab")
    place = (lax.axis_index("subset") % 2) * n_slab + lax.axis_index("slab")
    outside = ((hidden_slice == 0) & (place == 0)) | (
        (hidden_slice == hidden_count - 1) & (place == 2 * n_slab - 1)
    )
    return jnp.where(outside, 0.0, 1.0).astype(F32)


def weights_kernel(params_ref, first_ref, second_ref, turned_ref):
    params = params_ref[...]
    second = spread(params, second_column, False)
    first_ref[...] = spread(params, first_column, True)
    second_ref[...] = second
    turned_ref[...] = second.astype(F32).T.astype(BF16)


def weights(params):
    height = params.shape[0] * Y
    return pl.pallas_call(
        weights_kernel,
        out_shape=(
            jax.ShapeDtypeStruct((height, TILE), BF16),
            jax.ShapeDtypeStruct((height, TILE), BF16),
            jax.ShapeDtypeStruct((TILE, height), BF16),
        ),
        in_specs=[VMEM],
        out_specs=(VMEM,) * 3,
        compiler_params=vmem_mib(8),
        name="weights",
    )(params)


def join_kernel(mine_ref, came_ref, own_ref, shifted_ref):
    rows = mine_ref.shape[0]
    both = mine_ref[...] + came_ref[...]
    own_ref[...] = both[HALO : rows - HALO]
    fill_shifted(shifted_ref, both.reshape(rows * Y, X))


def join(mine, came):
    rows = mine.shape[0]
    return pl.pallas_call(
        join_kernel,
        out_shape=(
            jax.ShapeDtypeStruct((rows - 2 * HALO, Y, X), F32),
            jax.ShapeDtypeStruct((3, rows * Y, X), F32),
        ),
        in_specs=[VMEM] * 2,
        out_specs=(VMEM,) * 2,
        compiler_params=vmem_mib(8),
        name="join",
    )(mine, came)


def forward_kernel(
    shifted_ref, params_ref, first_ref, turned_ref, pred_ref, again_ref, hidden_ref, acc_ref
):
    rows = shifted_ref.shape[1] // Y
    hidden_count = rows - 2
    height = first_ref.shape[0]
    first = first_ref[...]
    acc_ref[...] = jnp.zeros(acc_ref.shape, F32)

    def one_slice(hidden_slice, carry):
        flag = slice_flag(hidden_slice, hidden_count)
        at = pl.multiple_of(hidden_slice * Y, Y)
        kept = pl.ds(pl.multiple_of(hidden_slice * height, height), height)
        for tile in range(X // TILE):
            cols = slice(tile * TILE, (tile + 1) * TILE)
            high, low = patch(shifted_ref, hidden_slice, tile)
            hidden = jnp.maximum(apply_spread(first, high, low), 0.0) * flag
            h_high, h_low = split2(hidden)
            hidden_ref[kept, cols] = h_high
            main = dot(turned_ref[BLOCK : 3 * BLOCK], h_high)
            taps = main[0:BLOCK] + main[BLOCK : 2 * BLOCK] + dot(turned_ref[0:BLOCK], h_low)
            for dx in range(3):
                acc_ref[dx, pl.ds(at, 3 * Y), cols] += taps[24 * dx : 24 * dx + 24]
        return carry

    lax.fori_loop(0, hidden_count, one_slice, 0, unroll=2)
    inner = slice(HALO * Y, (rows - HALO) * Y)
    added = acc_ref[1, inner, :]
    for dx in (0, 2):
        added = added + shift_columns(acc_ref[dx, inner, :], 1 - dx)
    own = shifted_ref[1, inner, :]
    bias = params_ref[0:1, B_SECOND_AT : B_SECOND_AT + 1]
    pred = (own + added + bias).reshape(pred_ref.shape)
    pred_ref[...] = pred
    again_ref[...] = pred


def forward(shifted, params, first, turned):
    rows = shifted.shape[1] // Y
    height = first.shape[0]
    own = jax.ShapeDtypeStruct((rows - 2 * HALO, Y, X), F32)
    return pl.pallas_call(
        forward_kernel,
        out_shape=(
            own,
            own,
            jax.ShapeDtypeStruct(((rows - 2) * height, X), BF16),
        ),
        in_specs=[VMEM] * 4,
        out_specs=(VMEM,) * 3,
        scratch_shapes=[pltpu.VMEM((3, rows * Y, X), F32)],
        cost_estimate=pl.CostEstimate(
            flops=20_000_000_000, bytes_accessed=2_000_000, transcendentals=0
        ),
        compiler_params=vmem_mib(18),
        name="forward",
    )(shifted, params, first, turned)


def backward_kernel(cells, others, shifted_ref, hidden_ref, pred_ref, second_ref, *refs):
    part_refs = refs[:others]
    out_ref, target_out_ref, grad_ref, acc1_ref, acc2_ref = refs[others:]
    rows = shifted_ref.shape[1] // Y
    hidden_count = rows - 2
    height = second_ref.shape[0]
    channels = height // Y
    target = part_refs[0][...]
    for part_ref in part_refs[1:]:
        target = target + part_ref[...]
    target = target if others == 1 else target / others
    target_out_ref[...] = target
    diff = (pred_ref[...] - target).reshape((rows - 2 * HALO) * Y, X)
    resid = 2.0 * diff / cells
    loss = jnp.sum(diff * diff, keepdims=True) / cells
    grad_b2 = jnp.sum(resid, keepdims=True)
    inner = slice(HALO * Y, (rows - HALO) * Y)
    for dx in range(3):
        grad_ref[dx, 0 : HALO * Y, :] = jnp.zeros((HALO * Y, X), F32)
        grad_ref[dx, (rows - HALO) * Y : rows * Y, :] = jnp.zeros((HALO * Y, X), F32)
        grad_ref[dx, inner, :] = shift_columns(resid, dx - 1)
    acc1_ref[...] = jnp.zeros(acc1_ref.shape, F32)
    acc2_ref[...] = jnp.zeros(acc2_ref.shape, F32)
    second = second_ref[...]

    def one_slice(hidden_slice, carry):
        kept = pl.ds(pl.multiple_of(hidden_slice * height, height), height)
        sum1 = None
        sum2 = None
        for tile in range(X // TILE):
            cols = slice(tile * TILE, (tile + 1) * TILE)
            high, low = patch(shifted_ref, hidden_slice, tile)
            g_high, g_low = patch(grad_ref, hidden_slice, tile)
            hidden = hidden_ref[kept, cols]
            grad_hidden = apply_spread(second, g_high, g_low)
            grad_pre = jnp.where(hidden.astype(F32) > 0.0, grad_hidden, 0.0).astype(BF16)
            part1 = dot_nt(grad_pre, jnp.concatenate([high, low], axis=0))
            part2 = dot_nt(hidden, jnp.concatenate([g_high, g_low], axis=0))
            sum1 = part1 if sum1 is None else sum1 + part1
            sum2 = part2 if sum2 is None else sum2 + part2
        acc1_ref[:, 0 : 2 * BLOCK] += sum1
        acc2_ref[:, 0 : 2 * BLOCK] += sum2
        return carry

    lax.fori_loop(0, hidden_count, one_slice, 0, unroll=2)

    def folded(ref):
        moved = pltpu.roll(ref[...], 2 * LANES - BLOCK, 1)
        return ref[:, 0:LANES] + moved[:, 0:LANES]

    total = gather_taps(
        ((folded(acc1_ref), first_column, True), (folded(acc2_ref), second_column, False)), channels
    )
    lane = iota((channels, LANES), 1)
    diagonal = lane == iota((channels, LANES), 0)
    line = jnp.sum(jnp.where(diagonal, total[:, TAPS : TAPS + 1], 0.0), axis=0, keepdims=True)
    line = jnp.where(lane[0:8] == LOSS_AT, loss, jnp.broadcast_to(line, (8, LANES)))
    out_ref[0:channels, :] = total
    out_ref[channels : channels + 8, :] = jnp.where(lane[0:8] == GRAD_B_SECOND_AT, grad_b2, line)


def backward(shifted, hidden, pred, parts, second, cells):
    height = second.shape[0]
    return pl.pallas_call(
        functools.partial(backward_kernel, cells, len(parts)),
        out_shape=(
            jax.ShapeDtypeStruct((height // Y + 8, LANES), F32),
            jax.ShapeDtypeStruct(pred.shape, F32),
        ),
        in_specs=[VMEM] * (4 + len(parts)),
        out_specs=(VMEM, VMEM),
        scratch_shapes=[
            pltpu.VMEM(shifted.shape, F32),
            pltpu.VMEM((height, 2 * LANES), F32),
            pltpu.VMEM((height, 2 * LANES), F32),
        ],
        compiler_params=vmem_mib(18),
        name="backward",
    )(shifted, hidden, pred, second, *parts)


def finish_kernel(one_ref, two_ref, loss_ref, w1_ref, b1_ref, w2_ref, b2_ref):
    total = one_ref[...] + two_ref[...]
    channels = w1_ref.shape[0]
    line = total[channels : channels + 1]
    loss_ref[...] = line[:, LOSS_AT : LOSS_AT + 1]
    w1_ref[...] = total[0:channels, 0:TAPS]
    b1_ref[...] = line[:, 0:channels]
    w2_ref[...] = total[0:channels, W_SECOND_AT : W_SECOND_AT + TAPS]
    b2_ref[...] = line[:, GRAD_B_SECOND_AT : GRAD_B_SECOND_AT + 1]


def sum_everywhere(value, channels):
    devices = lax.axis_size("subset") * lax.axis_size("slab")
    apart = 1
    while True:
        arrived = lax.ppermute(value, BOTH, [(i, i ^ apart) for i in range(devices)])
        apart *= 2
        if apart == devices:
            break
        value = value + arrived
    shapes = ((1, 1), (channels, TAPS), (1, channels), (channels, TAPS), (1, 1))
    return pl.pallas_call(
        finish_kernel,
        out_shape=tuple(jax.ShapeDtypeStruct(shape, F32) for shape in shapes),
        in_specs=[VMEM, VMEM],
        out_specs=(VMEM,) * 5,
        compiler_params=vmem_mib(1),
        name="finish",
    )(value, arrived)


def body(sinogram, angles, w_first, b_first, w_second, b_second):
    n_sub = lax.axis_size("subset") // 2
    n_slab = lax.axis_size("slab")
    devices = 2 * n_sub * n_slab
    group = 2 * n_slab
    local_views, z_count = sinogram.shape[0], sinogram.shape[1]
    depth = z_count // group
    channels = w_first.shape[0]
    scale = math.pi / (local_views * group)
    cells = float(n_sub * z_count * Y * X)
    assert devices & (devices - 1) == 0 and n_slab > 1 and channels == 32 and depth >= HALO

    sent = pack(angles, sinogram, n_slab, depth)

    def exchange(value, distance):
        return lax.ppermute(value, BOTH, [(i, i ^ distance) for i in range(devices)])

    arrived = [sent[0]] + [None] * (n_slab - 1)
    for distance in range(1, n_slab):
        arrived[distance] = exchange(sent[distance], distance)
    near = n_slab // 2 + 1
    sums = project(arrived[:near], (), 0.0)
    sums, w_first, b_first, w_second, b_second = lax.optimization_barrier(
        (sums, w_first, b_first, w_second, b_second)
    )
    params = jnp.concatenate(
        [
            w_first,
            b_first[:, None],
            jnp.zeros((channels, W_SECOND_AT - TAPS - 1), F32),
            w_second,
            jnp.broadcast_to(b_second, (channels, LANES - W_SECOND_AT - TAPS)),
        ],
        axis=1,
    )
    sums, (first, second, turned) = lax.optimization_barrier((sums, weights(params)))
    mine, other = project(arrived[near:], sums, scale)
    came = exchange(other, n_slab)
    own, shifted = join(mine, came)
    parts = []
    for apart in range(1, n_sub):
        pairs = [(i, (i + apart * group) % devices) for i in range(devices)]
        parts.append(lax.ppermute(own, BOTH, pairs))

    pred, again, hidden = forward(shifted, params, first, turned)
    partial, target = backward(shifted, hidden, again, parts, second, cells)
    loss, grad_w1, grad_b1, grad_w2, grad_b2 = sum_everywhere(partial, channels)
    return (
        pred[None],
        target[None],
        loss.reshape(()),
        grad_w1,
        grad_b1.reshape(-1),
        grad_w2,
        grad_b2.reshape(-1),
    )


def solution(mesh):
    return jax.shard_map(
        body,
        mesh=mesh,
        in_specs=(P(BOTH, None, None), P(BOTH), P(), P(), P(), P()),
        out_specs=(
            P("subset", "slab", None, None),
            P("subset", "slab", None, None),
            P(),
            P(),
            P(),
            P(),
            P(),
        ),
        check_vma=False,
    )
```
